32 devices in a mesh: groups: 2 (over y), space: 4 (over z), chan: 4 (over x, core).
Axes of the slice: x: 2, y: 2, z: 4, core: 2. Of those that a mesh axis runs over, the one named last changes fastest.
Arguments:
- inputs: bfloat16 [2, 128, 8, 1024], P('groups', 'chan', 'space'), parts along dimension 0, may hold values from -6 to 6
- pre_act: bfloat16 [2, 128, 8, 1024], P('groups', 'chan', 'space'), parts along dimension 0, may hold values from -6 to 6
- out_grad: bfloat16 [2, 256, 4, 256], P('groups', 'chan', 'space'), parts along dimension 0, may hold values from -12 to 12
- weight_one: bfloat16 [3, 3, 3, 128, 128], P(None, None, None, 'chan'), may hold values from -0.109375 to 0.109375
- weight_two: bfloat16 [3, 3, 3, 128, 256], P(None, None, None, 'chan'), may hold values from -0.109375 to 0.109375
Outputs:
- in_grad: bfloat16 [2, 128, 8, 1024], P('groups', 'chan', 'space'), parts along dimension 0
- filter_one_grad: float32 [6, 3, 3, 128, 128], P('groups', None, None, 'chan'), parts along dimension 0
- filter_two_grad: float32 [6, 3, 3, 128, 256], P('groups', None, None, 'chan'), parts along dimension 0
The draws below stay inside these ranges and needn't reach their ends.
There are 2 independent parts, one for each index of `groups`. The reference program is written for one: setup_inputs(seed, part) draws one part's arguments, and reference() takes and returns one part's arrays. A program takes and returns all parts, laid end to end along the dimension named above; an argument that names none is the same for every part. Nothing has to cross between parts.
All inputs are finite; a program needn't handle non-finite values.
Results may differ from the reference program's by a relative error of at most 0.0049.
Values may be sent and summed in bfloat16 or wider, within the bound.
A program may use at most 64 MiB of HBM per device.

```python
import math
import jax
import jax.numpy as jnp
from jax import lax

SAMPLES = 1
GRID = 32
CH = 128
CH2 = 256
DEPTH = 8
ODEPTH = 4
OGRID = 16


def shard_levels(own_key, shape, cuts, smallest, top_value):
    def one(dim, shards_of):
        steps = jax.random.uniform(jax.random.fold_in(jax.random.fold_in(own_key, 6), dim), (shards_of,), jnp.float32, smallest / len(cuts), top_value / len(cuts))
        return jnp.repeat(jnp.exp(steps), shape[dim] // shards_of).reshape((-1,) + (1,) * (len(shape) - dim - 1))

    factor_of = one(*cuts[0])
    for cut in cuts[1:]:
        factor_of = factor_of * one(*cut)
    return factor_of


def normal_values(stream_key, extent, width, most, shards=(), held_as=jnp.bfloat16):
    gain = shard_levels(stream_key, extent, shards, -0.22, 0.18) if shards else 1.0
    entries = jax.random.normal(stream_key, extent, jnp.float32) * width * gain
    return jnp.minimum(jnp.maximum(entries, -most), most).astype(held_as)


def setup_inputs(seed: int = 0, part: int = 0) -> dict:
    seeds = jax.random.split(jax.random.key(seed), 6)
    part_splits = jax.random.split(jax.random.fold_in(seeds[5], part), 6)
    inputs = normal_values(part_splits[0], (SAMPLES, CH, DEPTH, GRID * GRID), 1.0, 6.0, ((1, 4), (2, 4)))
    pre_act = normal_values(part_splits[1], (SAMPLES, CH, DEPTH, GRID * GRID), 1.0, 6.0, ((1, 4), (2, 4)))
    out_grad = normal_values(part_splits[2], (SAMPLES, CH2, ODEPTH, OGRID * OGRID), 2.0, 12.0, ((1, 4), (2, 4)))
    weight_one = normal_values(seeds[3], (3, 3, 3, CH, CH), (27 * CH) ** -0.5, 0.109375, ((3, 4),))
    weight_two = normal_values(seeds[4], (3, 3, 3, CH, CH2), (27 * CH) ** -0.5, 0.109375, ((3, 4),))
    return {"inputs": inputs, "pre_act": pre_act, "out_grad": out_grad, "weight_one": weight_one, "weight_two": weight_two}


leak_slope = 0.3
layout = ('NCDHW', 'DHWIO', 'NCDHW')

def conv_wide(field, kernel, padding, dilation):
    return lax.conv_general_dilated(field.astype(jnp.float32), kernel.astype(jnp.float32), (1, 1, 1), padding, lhs_dilation=dilation, dimension_numbers=layout, precision=lax.Precision.HIGHEST)

def filter_terms(source, grads, stride):
    counts = grads.shape[2:]
    leading = source.shape[:2]
    result = []
    for depth_tap in range(3):
        for row_tap in range(3):
            for col_tap in range(3):
                begin = (0, 0, depth_tap, row_tap, col_tap)
                finish = (leading[0], leading[1], depth_tap + stride * (counts[0] - 1) + 1, row_tap + stride * (counts[1] - 1) + 1, col_tap + stride * (counts[2] - 1) + 1)
                window = lax.slice(source, begin, finish, (1, 1, stride, stride, stride))
                result.append(jnp.einsum('bcdhw,bodhw->co', window.astype(jnp.float32), grads.astype(jnp.float32), precision=lax.Precision.HIGHEST))
    return jnp.stack(result).reshape(3, 3, 3, source.shape[1], grads.shape[1])

def reference(inputs, pre_act, out_grad, weight_one, weight_two):
    source = inputs.reshape(SAMPLES, CH, DEPTH, GRID, GRID)
    pre_value = pre_act.reshape(SAMPLES, CH, DEPTH, GRID, GRID).astype(jnp.float32)
    grads = out_grad.reshape(SAMPLES, CH2, ODEPTH, OGRID, OGRID)
    activation = jnp.where(pre_value > 0, pre_value, leak_slope * pre_value).astype(jnp.bfloat16)
    kernel_two = jnp.swapaxes(jnp.flip(weight_two, (0, 1, 2)), 3, 4)
    act_grad = conv_wide(grads, kernel_two, [(1, 2), (1, 2), (1, 2)], (2, 2, 2))
    pre_grad = jnp.where(pre_value > 0, act_grad, leak_slope * act_grad).astype(jnp.bfloat16)
    kernel_one = jnp.swapaxes(jnp.flip(weight_one, (0, 1, 2)), 3, 4)
    in_grad = conv_wide(pre_grad, kernel_one, [(1, 1), (1, 1), (1, 1)], (1, 1, 1)).astype(jnp.bfloat16)
    margins = ((0, 0), (0, 0), (1, 1), (1, 1), (1, 1))
    scale_one = 1.0 / math.sqrt(SAMPLES * DEPTH * GRID * GRID)
    scale_two = 1.0 / math.sqrt(SAMPLES * ODEPTH * OGRID * OGRID)
    filter_one_grad = filter_terms(jnp.pad(source, margins), pre_grad, 1) * scale_one
    filter_two_grad = filter_terms(jnp.pad(activation, margins), grads, 2) * scale_two
    return (in_grad.reshape(SAMPLES, CH, DEPTH, GRID * GRID), filter_one_grad, filter_two_grad)
```

```python
import functools
import math

import jax
import jax.numpy as jnp
from jax import lax
from jax.experimental import pallas as pl
from jax.experimental.pallas import tpu as pltpu
from jax.sharding import PartitionSpec as P

TAPS = 3
leak_slope = 0.3
MESH = pl.DeviceIdType.MESH
f32, bf16 = jnp.float32, jnp.bfloat16


def nt(a, b):
    return lax.dot_general(a, b, (((1,), (1,)), ((), ())), preferred_element_type=f32)


def nn(a, b):
    return jnp.dot(a, b, preferred_element_type=f32)


def lane_iota(shape):
    return lax.broadcasted_iota(jnp.int32, shape, 1)


def moved(value, row_step, col_step, side):
    length = value.shape[1]
    offset = row_step * side + col_step
    if offset % length:
        value = pltpu.roll(value, (-offset) % length, 1)
    lane = lane_iota((1, length))
    row, col = lane // side + row_step, lane % side + col_step
    if row_step or col_step:
        keep = (row >= 0) & (row < side) & (col >= 0) & (col < side)
        value = jnp.where(keep, value, 0.0)
    return value


def one_axis(shift):
    return [(0, 1), (1, 2)] if shift == 0 else [(1, 0)]


def combos():
    result = []
    for sd in range(2):
        for sh in range(2):
            for sw in range(2):
                pairs = []
                for d, kd in one_axis(sd):
                    for a, kh in one_axis(sh):
                        for b, kw in one_axis(sw):
                            pairs.append((d * 4 + a * 2 + b, (kd * TAPS + kh) * TAPS + kw))
                result.append((sd, sh, sw, pairs))
    return result


def kernel(nc, ns, side, scales, x_ref, h_ref, g_ref, w1_ref, w2_ref,
           in_ref, f1_ref, f2_ref,
           gbuf, gsh, hcls, dmat, pbuf, xs, s1, s2, r1, r2, o1, o2,
           g_sem, n_sem, p_sem, u_sem, d_sem, rs1_sem, rs2_sem, ag1_sem, ag2_sem):
    s, c = lax.axis_index("space"), lax.axis_index("chan")
    planes, ch, cells = x_ref.shape
    goc = g_ref.shape[0]
    oside = side // 2
    ocells = g_ref.shape[1]
    taps = s1.shape[0] // ns
    count = w1_ref.shape[0]

    def at_chan(t):
        return lax.rem(c + t, nc)

    def at_space(t):
        return lax.rem(s + t, ns)

    offsets = {(i % ns, j) for i in (-1, 0, 1) for j in range(nc)}
    offsets |= {(i, 0) for i in range(ns)}
    offsets = sorted(offsets - {(0, 0)})
    barrier = pltpu.get_barrier_semaphore()
    for i, j in offsets:
        pl.semaphore_signal(barrier, inc=1, device_id={"space": at_space(i), "chan": at_chan(j)}, device_id_type=MESH)
    pl.semaphore_wait(barrier, len(offsets))

    def remote(src, dst, sem, i, where):
        return pltpu.make_async_remote_copy(
            src_ref=src, dst_ref=dst, send_sem=sem.at[0, i], recv_sem=sem.at[1, i],
            device_id=where, device_id_type=MESH)

    g_rows = pl.ds(pl.multiple_of(c * goc, goc), goc)
    g_copies = [remote(g_ref, gbuf.at[0, g_rows], g_sem, t, {"chan": at_chan(t)}) for t in range(1, nc)]
    n_copies = [remote(g_ref, gbuf.at[1, g_rows], n_sem, t,
                       {"space": lax.max(s - 1, 0), "chan": at_chan(t)}) for t in range(nc)]
    for copy in g_copies:
        copy.start()

    @pl.when(s > 0)
    def _():
        for copy in n_copies:
            copy.start()

    gbuf[0, g_rows, :] = g_ref[...]

    @pl.when(s == ns - 1)
    def _():
        gbuf[1] = jnp.zeros(gbuf.shape[1:], bf16)
        pbuf[planes + 1] = jnp.zeros(pbuf.shape[1:], bf16)

    @pl.when(s == 0)
    def _():
        pbuf[0] = jnp.zeros(pbuf.shape[1:], bf16)

    size = dmat.shape[0]
    part = size // 4
    halves = cells // size
    lane = lane_iota((1, size))
    cls, inner = lane // part, lane % part
    target = (2 * (inner // oside) + cls // 2) * side + 2 * (inner % oside) + cls % 2
    dmat[...] = jnp.where(lax.broadcasted_iota(jnp.int32, (size, size), 0) == target, 1.0, 0.0).astype(bf16)
    for half in range(halves):
        block = jnp.concatenate([h_ref[d, :, half * size:(half + 1) * size] for d in range(planes)], axis=0)
        found = nn(block, dmat[...])
        for d in range(planes):
            for k in range(4):
                hcls[d * 4 + k, :, half * part:(half + 1) * part] = found[d * ch:(d + 1) * ch, k * part:(k + 1) * part]

    for copy in g_copies:
        copy.wait_recv()
    for sd in range(2):
        if sd == 1:
            @pl.when(s < ns - 1)
            def _():
                for copy in n_copies:
                    copy.wait_recv()
        field = gbuf[sd].astype(f32)
        for sh in range(2):
            for sw in range(2):
                gsh[sd * 4 + sh * 2 + sw] = moved(field, sh, sw, oside).astype(bf16)

    total = [None] * 8
    for index, (_, _, _, pairs) in enumerate(combos()):
        weights = jnp.concatenate([w2_ref[k] for _, k in pairs], axis=0)
        found = nn(weights, gsh[index])
        for place, (k, _) in enumerate(pairs):
            piece = found[place * ch:(place + 1) * ch]
            total[k] = piece if total[k] is None else total[k] + piece
    grads = [jnp.where(hcls[k] > 0, total[k], leak_slope * total[k]).astype(bf16) for k in range(8)]

    p_rows = pl.ds(pl.multiple_of(c * ch, ch), ch)
    for half in range(halves):
        block = jnp.concatenate([
            jnp.concatenate([grads[d * 4 + k][:, half * part:(half + 1) * part] for k in range(4)], axis=1)
            for d in range(planes)], axis=0)
        found = nt(block, dmat[...]).astype(bf16)
        for d in range(planes):
            pbuf[1 + d, p_rows, half * size:(half + 1) * size] = found[d * ch:(d + 1) * ch]

    mine = pbuf.at[pl.ds(1, planes), p_rows]
    p_copies = [remote(mine, mine, p_sem, t, {"chan": at_chan(t)}) for t in range(1, nc)]
    u_copies = [remote(pbuf.at[planes, p_rows], pbuf.at[0, p_rows], u_sem, t,
                       {"space": lax.min(s + 1, ns - 1), "chan": at_chan(t)}) for t in range(nc)]
    d_copies = [remote(pbuf.at[1, p_rows], pbuf.at[planes + 1, p_rows], d_sem, t,
                       {"space": lax.max(s - 1, 0), "chan": at_chan(t)}) for t in range(nc)]

    for copy in p_copies:
        copy.start()

    @pl.when(s < ns - 1)
    def _():
        for copy in u_copies:
            copy.start()

    @pl.when(s > 0)
    def _():
        for copy in d_copies:
            copy.start()

    act = [jnp.where(hcls[k] > 0, hcls[k], leak_slope * hcls[k]).astype(bf16) for k in range(8)]
    for index, (_, _, _, pairs) in enumerate(combos()):
        found = nt(jnp.concatenate([act[k] for k, _ in pairs], axis=0), gsh[index])
        for place, (_, k) in enumerate(pairs):
            s2[k] = found[place * ch:(place + 1) * ch].astype(bf16)
    for k in range(count, s2.shape[0]):
        s2[k] = jnp.zeros(s2.shape[1:], bf16)
        s1[k] = jnp.zeros(s1.shape[1:], bf16)

    def scatter(src, dst, sem):
        copies = [remote(src.at[pl.ds(at_space(t) * taps, taps)], dst.at[t], sem, t, {"space": at_space(t)})
                  for t in range(1, ns)]
        for copy in copies:
            copy.start()
        return copies

    own_taps = pl.ds(s * taps, taps)

    def reduce(src, dst, copies, out, scale, sem):
        value = src[own_taps].astype(f32)
        for t in range(1, ns):
            copies[t - 1].wait_recv()
            value = value + dst[t].astype(f32)
        out[own_taps] = (value * scale).astype(bf16)
        gathers = [remote(out.at[own_taps], out.at[own_taps], sem, t, {"space": at_space(t)}) for t in range(1, ns)]
        for copy in gathers:
            copy.start()
        return gathers

    rs2 = scatter(s2, r2, rs2_sem)

    for d in range(planes):
        field = x_ref[d].astype(f32)
        for kh in range(TAPS):
            for kw in range(TAPS):
                k = kh * TAPS + kw
                xs[d, k * ch:(k + 1) * ch, :] = moved(field, kh - 1, kw - 1, side).astype(bf16)

    for copy in p_copies:
        copy.wait_recv()

    @pl.when(s < ns - 1)
    def _():
        for copy in d_copies:
            copy.wait_recv()

    @pl.when(s > 0)
    def _():
        for copy in u_copies:
            copy.wait_recv()

    all_ch = pbuf.shape[1]
    found = None
    for d in range(planes):
        stack = pbuf[d:d + TAPS].reshape(TAPS * all_ch, cells)
        term = nt(xs[d], stack)
        found = term if found is None else found + term
    nine = TAPS * TAPS
    for kd in range(TAPS):
        column = (TAPS - 1 - kd) * all_ch
        for k in range(nine):
            s1[kd * nine + k] = found[k * ch:(k + 1) * ch, column:column + all_ch].astype(bf16)
    rs1 = scatter(s1, r1, rs1_sem)
    ag2 = reduce(s2, r2, rs2, o2, scales[1], ag2_sem)

    weights = jnp.concatenate(
        [w1_ref[kd * nine:(kd + 1) * nine].reshape(nine * ch, all_ch) for kd in reversed(range(TAPS))], axis=1)
    for d in range(planes):
        stack = pbuf[d:d + TAPS].reshape(TAPS * all_ch, cells)
        out = nn(weights, stack)
        result = None
        for kh in range(TAPS):
            rows = None
            for kw in range(TAPS):
                k = kh * TAPS + kw
                term = moved(out[k * ch:(k + 1) * ch], 0, 1 - kw, side)
                rows = term if rows is None else rows + term
            rows = moved(rows, 1 - kh, 0, side)
            result = rows if result is None else result + rows
        in_ref[d] = result.astype(bf16)

    ag1 = reduce(s1, r1, rs1, o1, scales[0], ag1_sem)
    for copy in ag2:
        copy.wait_recv()
    f2_ref[...] = o2[0:count].astype(f32)
    for copy in ag1:
        copy.wait_recv()
    f1_ref[...] = o1[0:count].astype(f32)

    for copy in g_copies + p_copies + rs1 + rs2 + ag1 + ag2:
        copy.wait_send()

    @pl.when(s > 0)
    def _():
        for copy in n_copies + d_copies:
            copy.wait_send()

    @pl.when(s < ns - 1)
    def _():
        for copy in u_copies:
            copy.wait_send()


def shards(nc, ns, inputs, pre_act, out_grad, weight_one, weight_two):
    samples, ch, planes, cells = inputs.shape
    goc, oplanes, ocells = out_grad.shape[1:]
    assert samples == 1 and planes == 2 and oplanes == 1
    side = math.isqrt(cells)
    count = TAPS ** 3
    x = jnp.swapaxes(inputs[0], 0, 1)
    h = jnp.swapaxes(pre_act[0], 0, 1)
    g = out_grad.reshape(goc, ocells)
    all_ch, all_goc = weight_one.shape[4], weight_two.shape[4]
    w1 = weight_one.reshape(count, ch, all_ch)
    w2 = weight_two.reshape(count, ch, all_goc)
    taps = -(-count // ns)
    size = min(cells, 4 * 128)
    scales = (1.0 / math.sqrt(samples * planes * ns * cells), 1.0 / math.sqrt(samples * oplanes * ns * ocells))
    vmem = pl.BlockSpec(memory_space=pltpu.VMEM)
    dma = pltpu.SemaphoreType.DMA
    out, one, two = pl.pallas_call(
        functools.partial(kernel, nc, ns, side, scales),
        out_shape=(
            jax.ShapeDtypeStruct((planes, ch, cells), bf16),
            jax.ShapeDtypeStruct((count, ch, all_ch), f32),
            jax.ShapeDtypeStruct((count, ch, all_goc), f32),
        ),
        in_specs=[vmem] * 5,
        out_specs=(vmem,) * 3,
        scratch_shapes=[
            pltpu.VMEM((2, all_goc, ocells), bf16),
            pltpu.VMEM((8, all_goc, ocells), bf16),
            pltpu.VMEM((8, ch, ocells), f32),
            pltpu.VMEM((size, size), bf16),
            pltpu.VMEM((planes + 2, all_ch, cells), bf16),
            pltpu.VMEM((planes, TAPS * TAPS * ch, cells), bf16),
            pltpu.VMEM((taps * ns, ch, all_ch), bf16),
            pltpu.VMEM((taps * ns, ch, all_goc), bf16),
            pltpu.VMEM((ns, taps, ch, all_ch), bf16),
            pltpu.VMEM((ns, taps, ch, all_goc), bf16),
            pltpu.VMEM((taps * ns, ch, all_ch), bf16),
            pltpu.VMEM((taps * ns, ch, all_goc), bf16),
            dma((2, nc)), dma((2, nc)), dma((2, nc)), dma((2, nc)), dma((2, nc)),
            dma((2, ns)), dma((2, ns)), dma((2, ns)), dma((2, ns)),
        ],
        compiler_params=pltpu.CompilerParams(
            collective_id=0, has_side_effects=True, vmem_limit_bytes=48 * 1024 * 1024),
    )(x, h, g, w1, w2)
    in_grad = jnp.swapaxes(out, 0, 1).reshape(inputs.shape)
    return (in_grad, one.reshape(TAPS, TAPS, TAPS, ch, all_ch), two.reshape(TAPS, TAPS, TAPS, ch, all_goc))


def solution(mesh):
    in_specs = (
        P("groups", "chan", "space", None),
        P("groups", "chan", "space", None),
        P("groups", "chan", "space", None),
        P(None, None, None, "chan", None),
        P(None, None, None, "chan", None),
    )
    out_specs = (
        P("groups", "chan", "space", None),
        P("groups", None, None, "chan", None),
        P("groups", None, None, "chan", None),
    )
    body = functools.partial(shards, mesh.shape["chan"], mesh.shape["space"])
    return jax.shard_map(body, mesh=mesh, in_specs=in_specs, out_specs=out_specs, check_vma=False)
```

```python
import functools
import math

import jax
import jax.numpy as jnp
from jax import lax
from jax.experimental import pallas as pl
from jax.experimental.pallas import tpu as pltpu
from jax.sharding import PartitionSpec as P

TAPS = 3
LINE = 4
CHUNKS = 4
leak_slope = 0.3
MESH = pl.DeviceIdType.MESH
f32, bf16 = jnp.float32, jnp.bfloat16


def nt(a, b):
    return lax.dot_general(a, b, (((1,), (1,)), ((), ())), preferred_element_type=f32)


def nn(a, b):
    return jnp.dot(a, b, preferred_element_type=f32)


def lane_iota(shape):
    return lax.broadcasted_iota(jnp.int32, shape, 1)


def moved(value, row_step, col_step, side):
    length = value.shape[1]
    offset = row_step * side + col_step
    if offset % length:
        value = pltpu.roll(value, (-offset) % length, 1)
    lane = lane_iota((1, length))
    row, col = lane // side + row_step, lane % side + col_step
    if row_step or col_step:
        keep = (row >= 0) & (row < side) & (col >= 0) & (col < side)
        value = jnp.where(keep, value, 0.0)
    return value


def one_axis(shift):
    return [(0, 1), (1, 2)] if shift == 0 else [(1, 0)]


def combos():
    result = []
    for sd in range(2):
        for sh in range(2):
            for sw in range(2):
                pairs = []
                for d, kd in one_axis(sd):
                    for a, kh in one_axis(sh):
                        for b, kw in one_axis(sw):
                            pairs.append((d * 4 + a * 2 + b, (kd * TAPS + kh) * TAPS + kw))
                result.append((sd, sh, sw, pairs))
    return result


def kernel(nc, ns, side, scales, x_ref, h_ref, g_ref, w1_ref, w2_ref,
           in_ref, f1_ref, f2_ref,
           gbuf, gsh, hcls, dmat, pbuf, xs, s1, s2, r1, r2, o1, o2, b1, b2,
           g_sem, n_sem, p_sem, u_sem, d_sem, a1_sem, a2_sem, c1_sem, c2_sem, m1_sem, m2_sem):
    s, c = lax.axis_index("space"), lax.axis_index("chan")
    planes, ch, cells = x_ref.shape
    goc = g_ref.shape[0]
    oside = side // 2
    ocells = g_ref.shape[1]
    count = w1_ref.shape[0]
    line = ns == LINE

    def at_chan(t):
        return lax.rem(c + t, nc)

    def at_space(t):
        return lax.rem(s + t, ns)

    offsets = {(i % ns, j) for i in (-1, 0, 1) for j in range(nc)}
    if not line:
        offsets |= {(i, 0) for i in range(ns)}
    offsets = sorted(offsets - {(0, 0)})
    barrier = pltpu.get_barrier_semaphore()
    for i, j in offsets:
        pl.semaphore_signal(barrier, inc=1, device_id={"space": at_space(i), "chan": at_chan(j)}, device_id_type=MESH)
    pl.semaphore_wait(barrier, len(offsets))

    def remote(src, dst, sem, i, where):
        return pltpu.make_async_remote_copy(
            src_ref=src, dst_ref=dst, send_sem=sem.at[0, i], recv_sem=sem.at[1, i],
            device_id=where, device_id_type=MESH)

    g_rows = pl.ds(pl.multiple_of(c * goc, goc), goc)
    g_copies = [remote(g_ref, gbuf.at[0, g_rows], g_sem, t, {"chan": at_chan(t)}) for t in range(1, nc)]
    n_copies = [remote(g_ref, gbuf.at[1, g_rows], n_sem, t,
                       {"space": lax.max(s - 1, 0), "chan": at_chan(t)}) for t in range(nc)]
    for copy in g_copies:
        copy.start()

    @pl.when(s > 0)
    def _():
        for copy in n_copies:
            copy.start()

    gbuf[0, g_rows, :] = g_ref[...]

    @pl.when(s == ns - 1)
    def _():
        gbuf[1] = jnp.zeros(gbuf.shape[1:], bf16)
        pbuf[planes + 1] = jnp.zeros(pbuf.shape[1:], bf16)

    @pl.when(s == 0)
    def _():
        pbuf[0] = jnp.zeros(pbuf.shape[1:], bf16)

    size = dmat.shape[0]
    part = size // 4
    halves = cells // size
    lane = lane_iota((1, size))
    cls, inner = lane // part, lane % part
    target = (2 * (inner // oside) + cls // 2) * side + 2 * (inner % oside) + cls % 2
    dmat[...] = jnp.where(lax.broadcasted_iota(jnp.int32, (size, size), 0) == target, 1.0, 0.0).astype(bf16)
    for half in range(halves):
        block = jnp.concatenate([h_ref[d, :, half * size:(half + 1) * size] for d in range(planes)], axis=0)
        found = nn(block, dmat[...])
        for d in range(planes):
            for k in range(4):
                hcls[d * 4 + k, :, half * part:(half + 1) * part] = found[d * ch:(d + 1) * ch, k * part:(k + 1) * part]

    for copy in g_copies:
        copy.wait_recv()
    for sd in range(2):
        if sd == 1:
            @pl.when(s < ns - 1)
            def _():
                for copy in n_copies:
                    copy.wait_recv()
        field = gbuf[sd].astype(f32)
        for sh in range(2):
            for sw in range(2):
                gsh[sd * 4 + sh * 2 + sw] = moved(field, sh, sw, oside).astype(bf16)

    total = [None] * 8
    for index, (_, _, _, pairs) in enumerate(combos()):
        weights = jnp.concatenate([w2_ref[k] for _, k in pairs], axis=0)
        found = nn(weights, gsh[index])
        for place, (k, _) in enumerate(pairs):
            piece = found[place * ch:(place + 1) * ch]
            total[k] = piece if total[k] is None else total[k] + piece
    grads = [jnp.where(hcls[k] > 0, total[k], leak_slope * total[k]).astype(bf16) for k in range(8)]

    def rows_of(index):
        return pl.ds(pl.multiple_of(index * ch, ch), ch)

    p_rows = rows_of(c)
    for half in range(halves):
        block = jnp.concatenate([
            jnp.concatenate([grads[d * 4 + k][:, half * part:(half + 1) * part] for k in range(4)], axis=1)
            for d in range(planes)], axis=0)
        found = nt(block, dmat[...]).astype(bf16)
        for d in range(planes):
            pbuf[1 + d, p_rows, half * size:(half + 1) * size] = found[d * ch:(d + 1) * ch]

    u_copy = remote(pbuf.at[planes, p_rows], pbuf.at[0, p_rows], u_sem, 0, {"space": lax.min(s + 1, ns - 1)})
    d_copy = remote(pbuf.at[1, p_rows], pbuf.at[planes + 1, p_rows], d_sem, 0, {"space": lax.max(s - 1, 0)})

    class Spread:
        def __init__(self, where, sem):
            def block(index):
                return pbuf.at[where, rows_of(index)]

            mine = block(c)
            if nc == 4:
                near, far = c + 1 - 2 * lax.rem(c, 2), lax.rem(c + 2, nc)
                self.far = remote(mine, mine, sem, 2, {"chan": far})
                self.near = remote(mine, mine, sem, 1, {"chan": near})
                self.onward = remote(block(far), block(far), sem, 3, {"chan": near})
                self.first, self.all = [self.far, self.near], [self.far, self.near, self.onward]
            else:
                self.onward = None
                self.first = self.all = [remote(mine, mine, sem, t, {"chan": at_chan(t)}) for t in range(1, nc)]

        def start(self):
            for copy in self.first:
                copy.start()

        def forward(self):
            if self.onward is not None:
                self.far.wait_recv()
                self.onward.start()

        def wait_recv(self):
            for copy in self.all if self.onward is None else [self.near, self.onward]:
                copy.wait_recv()

        def wait_send(self):
            for copy in self.all:
                copy.wait_send()

    p_spread = Spread(pl.ds(1, planes), p_sem)
    u_spread = Spread(0, u_sem)
    d_spread = Spread(planes + 1, d_sem)
    below, above = s > 0, s < ns - 1

    pl.when(above)(u_copy.start)
    pl.when(below)(d_copy.start)
    p_spread.start()

    act = [jnp.where(hcls[k] > 0, hcls[k], leak_slope * hcls[k]).astype(bf16) for k in range(8)]
    for index, (_, _, _, pairs) in enumerate(combos()):
        found = nt(jnp.concatenate([act[k] for k, _ in pairs], axis=0), gsh[index])
        for place, (_, k) in enumerate(pairs):
            s2[k] = found[place * ch:(place + 1) * ch].astype(bf16)
    for k in range(count, s2.shape[0]):
        s2[k] = jnp.zeros(s2.shape[1:], bf16)
        s1[k] = jnp.zeros(s1.shape[1:], bf16)

    step = -(-count // (CHUNKS if line else ns))
    pieces = [(i, min(step, count - i)) for i in range(0, count, step)]

    class Sum:
        def __init__(self, src, got, mid, out, scale, sems):
            self.src, self.got, self.mid, self.out, self.scale = src, got, mid, out, scale
            self.sems = sems
            if line:
                inner, end, mate = 1 + s // (ns - 1), (ns - 1) * (s // 2), ns - 1 - s
                self.up, self.across, self.down = [], [], []
                for k, (i, n) in enumerate(pieces):
                    part, later = pl.ds(i, n), pl.ds(count + i, n)
                    self.up.append(remote(src.at[part], got.at[part], sems[0], k, {"space": inner}))
                    self.across.append(remote(mid.at[part], got.at[later], sems[1], k, {"space": mate}))
                    self.down.append(remote(out.at[part], out.at[part], sems[2], k, {"space": end}))
            else:
                own = pl.ds(s * step, step)
                self.scatters = [remote(src.at[pl.ds(at_space(t) * step, step)], got.at[pl.ds(t * step, step)],
                                        sems[0], t, {"space": at_space(t)}) for t in range(1, ns)]
                self.gathers = [remote(out.at[own], out.at[own], sems[2], t, {"space": at_space(t)})
                                for t in range(1, ns)]

        def first(self):
            if line:
                @pl.when(outer)
                def _():
                    for copy in self.up:
                        copy.start()
            else:
                for copy in self.scatters:
                    copy.start()

        def second(self):
            if line:
                @pl.when(jnp.logical_not(outer))
                def _():
                    for (i, n), up, across in zip(pieces, self.up, self.across):
                        up.wait_recv()
                        value = self.src[i:i + n].astype(f32) + self.got[i:i + n].astype(f32)
                        self.mid[i:i + n] = value.astype(bf16)
                        across.start()

        def third(self):
            if line:
                @pl.when(jnp.logical_not(outer))
                def _():
                    for (i, n), across, down in zip(pieces, self.across, self.down):
                        across.wait_recv()
                        value = self.mid[i:i + n].astype(f32) + self.got[count + i:count + i + n].astype(f32)
                        self.out[i:i + n] = (value * self.scale).astype(bf16)
                        down.start()
            else:
                own = pl.ds(s * step, step)
                value = self.src[own].astype(f32)
                for t, copy in enumerate(self.scatters, 1):
                    copy.wait_recv()
                    value = value + self.got[t * step:(t + 1) * step].astype(f32)
                self.out[own] = (value * self.scale).astype(bf16)
                for copy in self.gathers:
                    copy.start()

        def last(self):
            if line:
                @pl.when(outer)
                def _():
                    for copy in self.down:
                        copy.wait_recv()
            else:
                for copy in self.gathers:
                    copy.wait_recv()

        def wait_send(self):
            if line:
                @pl.when(outer)
                def _():
                    for copy in self.up:
                        copy.wait_send()

                @pl.when(jnp.logical_not(outer))
                def _():
                    for copy in self.across + self.down:
                        copy.wait_send()
            else:
                for copy in self.scatters + self.gathers:
                    copy.wait_send()

    outer = (s == 0) | (s == ns - 1)
    sum2 = Sum(s2, r2, b2, o2, scales[1], (a2_sem, m2_sem, c2_sem))
    sum1 = Sum(s1, r1, b1, o1, scales[0], (a1_sem, m1_sem, c1_sem))
    sum2.first()

    @pl.when(below)
    def _():
        u_copy.wait_recv()
        u_spread.start()

    @pl.when(above)
    def _():
        d_copy.wait_recv()
        d_spread.start()

    for d in range(planes):
        field = x_ref[d].astype(f32)
        for kh in range(TAPS):
            for kw in range(TAPS):
                k = kh * TAPS + kw
                xs[d, k * ch:(k + 1) * ch, :] = moved(field, kh - 1, kw - 1, side).astype(bf16)

    p_spread.forward()

    @pl.when(below)
    def _():
        u_spread.forward()

    @pl.when(above)
    def _():
        d_spread.forward()

    p_spread.wait_recv()

    @pl.when(below)
    def _():
        u_spread.wait_recv()

    @pl.when(above)
    def _():
        d_spread.wait_recv()

    all_ch = pbuf.shape[1]
    found = None
    for d in range(planes):
        stack = pbuf[d:d + TAPS].reshape(TAPS * all_ch, cells)
        term = nt(xs[d], stack)
        found = term if found is None else found + term
    nine = TAPS * TAPS
    for kd in range(TAPS):
        column = (TAPS - 1 - kd) * all_ch
        for k in range(nine):
            s1[kd * nine + k] = found[k * ch:(k + 1) * ch, column:column + all_ch].astype(bf16)
    sum1.first()
    sum2.second()

    weights = jnp.concatenate(
        [w1_ref[kd * nine:(kd + 1) * nine].reshape(nine * ch, all_ch) for kd in reversed(range(TAPS))], axis=1)
    for d in range(planes):
        stack = pbuf[d:d + TAPS].reshape(TAPS * all_ch, cells)
        out = nn(weights, stack)
        result = None
        for kh in range(TAPS):
            rows = None
            for kw in range(TAPS):
                k = kh * TAPS + kw
                term = moved(out[k * ch:(k + 1) * ch], 0, 1 - kw, side)
                rows = term if rows is None else rows + term
            rows = moved(rows, 1 - kh, 0, side)
            result = rows if result is None else result + rows
        in_ref[d] = result.astype(bf16)

    sum2.third()
    sum1.second()
    sum1.third()
    sum2.last()
    f2_ref[...] = o2[0:count].astype(f32)
    sum1.last()
    f1_ref[...] = o1[0:count].astype(f32)

    for item in g_copies + [p_spread, sum1, sum2]:
        item.wait_send()

    @pl.when(below)
    def _():
        for item in n_copies + [d_copy, u_spread]:
            item.wait_send()

    @pl.when(above)
    def _():
        for item in [u_copy, d_spread]:
            item.wait_send()


def shards(nc, ns, inputs, pre_act, out_grad, weight_one, weight_two):
    samples, ch, planes, cells = inputs.shape
    goc, oplanes, ocells = out_grad.shape[1:]
    assert samples == 1 and planes == 2 and oplanes == 1
    side = math.isqrt(cells)
    count = TAPS ** 3
    x = jnp.swapaxes(inputs[0], 0, 1)
    h = jnp.swapaxes(pre_act[0], 0, 1)
    g = out_grad.reshape(goc, ocells)
    all_ch, all_goc = weight_one.shape[4], weight_two.shape[4]
    w1 = weight_one.reshape(count, ch, all_ch)
    w2 = weight_two.reshape(count, ch, all_goc)
    line = ns == LINE
    spread = count if line else -(-count // ns) * ns
    got = 2 * count if line else spread
    lanes = max(ns, CHUNKS)
    size = min(cells, 4 * 128)
    scales = (1.0 / math.sqrt(samples * planes * ns * cells), 1.0 / math.sqrt(samples * oplanes * ns * ocells))
    vmem = pl.BlockSpec(memory_space=pltpu.VMEM)
    dma = pltpu.SemaphoreType.DMA
    out, one, two = pl.pallas_call(
        functools.partial(kernel, nc, ns, side, scales),
        out_shape=(
            jax.ShapeDtypeStruct((planes, ch, cells), bf16),
            jax.ShapeDtypeStruct((count, ch, all_ch), f32),
            jax.ShapeDtypeStruct((count, ch, all_goc), f32),
        ),
        in_specs=[vmem] * 5,
        out_specs=(vmem,) * 3,
        scratch_shapes=[
            pltpu.VMEM((2, all_goc, ocells), bf16),
            pltpu.VMEM((8, all_goc, ocells), bf16),
            pltpu.VMEM((8, ch, ocells), f32),
            pltpu.VMEM((size, size), bf16),
            pltpu.VMEM((planes + 2, all_ch, cells), bf16),
            pltpu.VMEM((planes, TAPS * TAPS * ch, cells), bf16),
            pltpu.VMEM((spread, ch, all_ch), bf16),
            pltpu.VMEM((spread, ch, all_goc), bf16),
            pltpu.VMEM((got, ch, all_ch), bf16),
            pltpu.VMEM((got, ch, all_goc), bf16),
            pltpu.VMEM((spread, ch, all_ch), bf16),
            pltpu.VMEM((spread, ch, all_goc), bf16),
            pltpu.VMEM((spread, ch, all_ch), bf16),
            pltpu.VMEM((spread, ch, all_goc), bf16),
            dma((2, nc)), dma((2, nc)), dma((2, nc)), dma((2, nc)), dma((2, nc)),
            dma((2, lanes)), dma((2, lanes)), dma((2, lanes)), dma((2, lanes)), dma((2, lanes)), dma((2, lanes)),
        ],
        compiler_params=pltpu.CompilerParams(
            collective_id=0, has_side_effects=True, vmem_limit_bytes=48 * 1024 * 1024),
    )(x, h, g, w1, w2)
    in_grad = jnp.swapaxes(out, 0, 1).reshape(inputs.shape)
    return (in_grad, one.reshape(TAPS, TAPS, TAPS, ch, all_ch), two.reshape(TAPS, TAPS, TAPS, ch, all_goc))


def solution(mesh):
    in_specs = (
        P("groups", "chan", "space", None),
        P("groups", "chan", "space", None),
        P("groups", "chan", "space", None),
        P(None, None, None, "chan", None),
        P(None, None, None, "chan", None),
    )
    out_specs = (
        P("groups", "chan", "space", None),
        P("groups", None, None, "chan", None),
        P("groups", None, None, "chan", None),
    )
    body = functools.partial(shards, mesh.shape["chan"], mesh.shape["space"])
    return jax.shard_map(body, mesh=mesh, in_specs=in_specs, out_specs=out_specs, check_vma=False)
```

```python
import functools
import math

import jax
import jax.numpy as jnp
from jax import lax
from jax.experimental import pallas as pl
from jax.experimental.pallas import tpu as pltpu
from jax.sharding import PartitionSpec as P

TAPS = 3
LINE = 4
CHUNKS = 9
leak_slope = 0.3
MESH = pl.DeviceIdType.MESH
f32, bf16 = jnp.float32, jnp.bfloat16


def nt(a, b):
    return lax.dot_general(a, b, (((1,), (1,)), ((), ())), preferred_element_type=f32)


def nn(a, b):
    return jnp.dot(a, b, preferred_element_type=f32)


def lane_iota(shape):
    return lax.broadcasted_iota(jnp.int32, shape, 1)


def moved(value, row_step, col_step, side):
    length = value.shape[1]
    offset = row_step * side + col_step
    if offset % length:
        value = pltpu.roll(value, (-offset) % length, 1)
    lane = lane_iota((1, length))
    row, col = lane // side + row_step, lane % side + col_step
    if row_step or col_step:
        keep = (row >= 0) & (row < side) & (col >= 0) & (col < side)
        value = jnp.where(keep, value, 0.0)
    return value


def one_axis(shift):
    return [(0, 1), (1, 2)] if shift == 0 else [(1, 0)]


def combos():
    result = []
    for sd in range(2):
        for sh in range(2):
            for sw in range(2):
                pairs = []
                for d, kd in one_axis(sd):
                    for a, kh in one_axis(sh):
                        for b, kw in one_axis(sw):
                            pairs.append((d * 4 + a * 2 + b, (kd * TAPS + kh) * TAPS + kw))
                result.append((sd, sh, sw, pairs))
    return result


def kernel(nc, ns, side, scales, x_ref, h_ref, g_ref, w1_ref, w2_ref,
           in_ref, f1_ref, f2_ref,
           gbuf, gsh, hcls, dmat, pbuf, xs, s1, s2, r1, r2, o1, o2, b1, b2,
           g_sem, n_sem, p_sem, u_sem, d_sem, a1_sem, a2_sem, c1_sem, c2_sem, m1_sem, m2_sem,
           hall, gall, gwide, awide, r_sem, l_sem, o_sem, os_sem):
    s, c = lax.axis_index("space"), lax.axis_index("chan")
    planes, ch, cells = x_ref.shape
    goc = g_ref.shape[0]
    oside = side // 2
    ocells = g_ref.shape[1]
    count = w1_ref.shape[0]
    line = ns == LINE

    def at_chan(t):
        return lax.rem(c + t, nc)

    def at_space(t):
        return lax.rem(s + t, ns)

    offsets = {(i % ns, j) for i in (-1, 0, 1) for j in range(nc)}
    offsets |= {(i, 0) for i in range(ns)}
    offsets = sorted(offsets - {(0, 0)})
    barrier = pltpu.get_barrier_semaphore()
    for i, j in offsets:
        pl.semaphore_signal(barrier, inc=1, device_id={"space": at_space(i), "chan": at_chan(j)}, device_id_type=MESH)
    if line:
        hall[s] = h_ref[...]

    @pl.when(s == ns - 1)
    def _():
        gbuf[1] = jnp.zeros(gbuf.shape[1:], bf16)
        pbuf[planes + 1] = jnp.zeros(pbuf.shape[1:], bf16)

    @pl.when(s == 0)
    def _():
        pbuf[0] = jnp.zeros(pbuf.shape[1:], bf16)

    size = dmat.shape[0]
    part = size // 4
    halves = cells // size
    lane = lane_iota((1, size))
    cls, inner = lane // part, lane % part
    target = (2 * (inner // oside) + cls // 2) * side + 2 * (inner % oside) + cls % 2
    dmat[...] = jnp.where(lax.broadcasted_iota(jnp.int32, (size, size), 0) == target, 1.0, 0.0).astype(bf16)
    for half in range(halves):
        block = jnp.concatenate([h_ref[d, :, half * size:(half + 1) * size] for d in range(planes)], axis=0)
        found = nn(block, dmat[...])
        for d in range(planes):
            for k in range(4):
                hcls[d * 4 + k, :, half * part:(half + 1) * part] = found[d * ch:(d + 1) * ch, k * part:(k + 1) * part]

    for d in range(planes):
        field = x_ref[d].astype(f32)
        for kh in range(TAPS):
            for kw in range(TAPS):
                k = kh * TAPS + kw
                xs[d, k * ch:(k + 1) * ch, :] = moved(field, kh - 1, kw - 1, side).astype(bf16)

    pl.semaphore_wait(barrier, len(offsets))

    def remote(src, dst, sem, i, where):
        return pltpu.make_async_remote_copy(
            src_ref=src, dst_ref=dst, send_sem=sem.at[0, i], recv_sem=sem.at[1, i],
            device_id=where, device_id_type=MESH)

    class Spread:
        def __init__(self, field, where, rows, sem, base=0):
            def block(index):
                return field.at[where, pl.ds(pl.multiple_of(index * rows, rows), rows)]

            mine = block(c)
            if nc == 4:
                near, far = c + 1 - 2 * lax.rem(c, 2), lax.rem(c + 2, nc)
                self.far = remote(mine, mine, sem, base + 2, {"chan": far})
                self.near = remote(mine, mine, sem, base + 1, {"chan": near})
                self.onward = remote(block(far), block(far), sem, base + 3, {"chan": near})
                self.first, self.all = [self.far, self.near], [self.far, self.near, self.onward]
            else:
                self.onward = None
                self.first = self.all = [remote(mine, mine, sem, base + t, {"chan": at_chan(t)}) for t in range(1, nc)]

        def start(self):
            for copy in self.first:
                copy.start()

        def forward(self):
            if self.onward is not None:
                self.far.wait_recv()
                self.onward.start()

        def wait_recv(self):
            for copy in self.all if self.onward is None else [self.near, self.onward]:
                copy.wait_recv()

        def wait_send(self):
            for copy in self.all:
                copy.wait_send()

    g_rows = pl.ds(pl.multiple_of(c * goc, goc), goc)
    g_copies = [remote(g_ref, gbuf.at[0, g_rows], g_sem, t, {"chan": at_chan(t)}) for t in range(1, nc)]
    n_copies = [remote(g_ref, gbuf.at[1, g_rows], n_sem, t,
                       {"space": lax.max(s - 1, 0), "chan": at_chan(t)}) for t in range(nc)]
    for copy in g_copies:
        copy.start()

    @pl.when(s > 0)
    def _():
        for copy in n_copies:
            copy.start()

    gbuf[0, g_rows, :] = g_ref[...]

    if line:
        to_next, to_last = {"space": lax.min(s + 1, ns - 1)}, {"space": lax.max(s - 1, 0)}
        right, left = [], []
        for j in range(ns - 1):
            block = hall.at[lax.max(s - j, 0)]
            right.append(remote(h_ref if j == 0 else block, block, r_sem, j, to_next))
            block = hall.at[lax.min(s + j, ns - 1)]
            left.append(remote(h_ref if j == 0 else block, block, l_sem, j, to_last))
        others = [remote(g_ref, gall.at[s, g_rows], o_sem, j, {"space": at_space(ns - j)}) for j in range(1, ns)]

        def has(j, other):
            return None if j > 1 else (s == 0 if not other else s == ns - 1)

        def maybe(cond, run):
            if cond is None:
                run()
            else:
                pl.when(cond)(run)

        for j in range(1, ns):
            maybe(has(j, False), others[j - 1].start)
        pl.when(s < ns - 1)(right[0].start)
        pl.when(s > 0)(left[0].start)

        def pass_on(j):
            @pl.when(s >= j)
            def _():
                right[j - 1].wait_recv()

            @pl.when(s <= ns - 1 - j)
            def _():
                left[j - 1].wait_recv()

            if j < ns - 1:
                pl.when((s >= j) & (s < ns - 1))(right[j].start)
                pl.when((s <= ns - 1 - j) & (s > 0))(left[j].start)

    for copy in g_copies:
        copy.wait_recv()
    for sd in range(2):
        if sd == 1:
            @pl.when(s < ns - 1)
            def _():
                for copy in n_copies:
                    copy.wait_recv()
        field = gbuf[sd].astype(f32)
        for sh in range(2):
            for sw in range(2):
                gsh[sd * 4 + sh * 2 + sw] = moved(field, sh, sw, oside).astype(bf16)

    total = [None] * 8
    for index, (_, _, _, pairs) in enumerate(combos()):
        weights = jnp.concatenate([w2_ref[k] for _, k in pairs], axis=0)
        found = nn(weights, gsh[index])
        for place, (k, _) in enumerate(pairs):
            piece = found[place * ch:(place + 1) * ch]
            total[k] = piece if total[k] is None else total[k] + piece
    grads = [jnp.where(hcls[k] > 0, total[k], leak_slope * total[k]).astype(bf16) for k in range(8)]

    def rows_of(index):
        return pl.ds(pl.multiple_of(index * ch, ch), ch)

    p_rows = rows_of(c)
    for half in range(halves):
        block = jnp.concatenate([
            jnp.concatenate([grads[d * 4 + k][:, half * part:(half + 1) * part] for k in range(4)], axis=1)
            for d in range(planes)], axis=0)
        found = nt(block, dmat[...]).astype(bf16)
        for d in range(planes):
            pbuf[1 + d, p_rows, half * size:(half + 1) * size] = found[d * ch:(d + 1) * ch]

    u_copy = remote(pbuf.at[planes, p_rows], pbuf.at[0, p_rows], u_sem, 0, {"space": lax.min(s + 1, ns - 1)})
    d_copy = remote(pbuf.at[1, p_rows], pbuf.at[planes + 1, p_rows], d_sem, 0, {"space": lax.max(s - 1, 0)})

    p_spread = Spread(pbuf, pl.ds(1, planes), ch, p_sem)
    u_spread = Spread(pbuf, 0, ch, u_sem)
    d_spread = Spread(pbuf, planes + 1, ch, d_sem)
    below, above = s > 0, s < ns - 1

    pl.when(above)(u_copy.start)
    pl.when(below)(d_copy.start)
    p_spread.start()

    if line:
        wide = [Spread(gall, lax.rem(s + j, ns), goc, os_sem, j * nc) for j in range(1, ns)]
        for j in range(1, ns):
            def relay(j=j):
                others[j - 1].wait_recv()
                wide[j - 1].start()

            maybe(has(j, True), relay)
        gall[s] = gbuf[0]

        @pl.when(s < ns - 1)
        def _():
            gall[lax.min(s + 1, ns - 1)] = gbuf[1]

    if not line:
        act = [jnp.where(hcls[k] > 0, hcls[k], leak_slope * hcls[k]).astype(bf16) for k in range(8)]
        for index, (_, _, _, pairs) in enumerate(combos()):
            found = nt(jnp.concatenate([act[k] for k, _ in pairs], axis=0), gsh[index])
            for place, (_, k) in enumerate(pairs):
                s2[k] = found[place * ch:(place + 1) * ch].astype(bf16)
    for k in range(count, s1.shape[0]):
        if not line:
            s2[k] = jnp.zeros(s2.shape[1:], bf16)
        s1[k] = jnp.zeros(s1.shape[1:], bf16)

    step = -(-count // (CHUNKS if line else ns))
    pieces = [(i, min(step, count - i)) for i in range(0, count, step)]

    class Sum:
        def __init__(self, src, got, mid, out, scale, sems):
            self.src, self.got, self.mid, self.out, self.scale = src, got, mid, out, scale
            self.sems = sems
            if line:
                inner, end, mate = 1 + s // (ns - 1), (ns - 1) * (s // 2), ns - 1 - s
                self.up, self.across, self.down = [], [], []
                for k, (i, n) in enumerate(pieces):
                    part, later = pl.ds(i, n), pl.ds(count + i, n)
                    self.up.append(remote(src.at[part], got.at[part], sems[0], k, {"space": inner}))
                    self.across.append(remote(mid.at[part], got.at[later], sems[1], k, {"space": mate}))
                    self.down.append(remote(out.at[part], out.at[part], sems[2], k, {"space": end}))
            else:
                own = pl.ds(s * step, step)
                self.scatters = [remote(src.at[pl.ds(at_space(t) * step, step)], got.at[pl.ds(t * step, step)],
                                        sems[0], t, {"space": at_space(t)}) for t in range(1, ns)]
                self.gathers = [remote(out.at[own], out.at[own], sems[2], t, {"space": at_space(t)})
                                for t in range(1, ns)]

        def first(self):
            if line:
                @pl.when(outer)
                def _():
                    for copy in self.up:
                        copy.start()
            else:
                for copy in self.scatters:
                    copy.start()

        def second(self):
            if line:
                @pl.when(jnp.logical_not(outer))
                def _():
                    for (i, n), up, across in zip(pieces, self.up, self.across):
                        up.wait_recv()
                        value = self.src[i:i + n].astype(f32) + self.got[i:i + n].astype(f32)
                        self.mid[i:i + n] = value.astype(bf16)
                        across.start()

        def third(self):
            if line:
                @pl.when(jnp.logical_not(outer))
                def _():
                    for (i, n), across, down in zip(pieces, self.across, self.down):
                        across.wait_recv()
                        value = self.mid[i:i + n].astype(f32) + self.got[count + i:count + i + n].astype(f32)
                        self.out[i:i + n] = (value * self.scale).astype(bf16)
                        down.start()
            else:
                own = pl.ds(s * step, step)
                value = self.src[own].astype(f32)
                for t, copy in enumerate(self.scatters, 1):
                    copy.wait_recv()
                    value = value + self.got[t * step:(t + 1) * step].astype(f32)
                self.out[own] = (value * self.scale).astype(bf16)
                for copy in self.gathers:
                    copy.start()

        def last(self):
            if line:
                @pl.when(outer)
                def _():
                    for copy in self.down:
                        copy.wait_recv()
            else:
                for copy in self.gathers:
                    copy.wait_recv()

        def wait_send(self):
            if line:
                @pl.when(outer)
                def _():
                    for copy in self.up:
                        copy.wait_send()

                @pl.when(jnp.logical_not(outer))
                def _():
                    for copy in self.across + self.down:
                        copy.wait_send()
            else:
                for copy in self.scatters + self.gathers:
                    copy.wait_send()

    outer = (s == 0) | (s == ns - 1)
    sum2 = None if line else Sum(s2, r2, b2, o2, scales[1], (a2_sem, m2_sem, c2_sem))
    sum1 = Sum(s1, r1, b1, o1, scales[0], (a1_sem, m1_sem, c1_sem))
    if line:
        pass_on(1)
    else:
        sum2.first()

    @pl.when(below)
    def _():
        u_copy.wait_recv()
        u_spread.start()

    @pl.when(above)
    def _():
        d_copy.wait_recv()
        d_spread.start()

    p_spread.forward()
    if line:
        for j in range(1, ns):
            maybe(has(j, True), wide[j - 1].forward)
        pass_on(2)

    @pl.when(below)
    def _():
        u_spread.forward()

    @pl.when(above)
    def _():
        d_spread.forward()

    p_spread.wait_recv()

    @pl.when(below)
    def _():
        u_spread.wait_recv()

    @pl.when(above)
    def _():
        d_spread.wait_recv()

    all_ch = pbuf.shape[1]
    found = None
    for d in range(planes):
        stack = pbuf[d:d + TAPS].reshape(TAPS * all_ch, cells)
        term = nt(xs[d], stack)
        found = term if found is None else found + term
    nine = TAPS * TAPS
    for kd in range(TAPS):
        column = (TAPS - 1 - kd) * all_ch
        for k in range(nine):
            s1[kd * nine + k] = found[k * ch:(k + 1) * ch, column:column + all_ch].astype(bf16)
    sum1.first()

    if line:
        pass_on(ns - 1)
        for j in range(1, ns):
            maybe(has(j, True), wide[j - 1].wait_recv)
        for p in range(ns):
            field = gall[p].astype(f32)
            for sh in range(2):
                for sw in range(2):
                    gwide[sh * 2 + sw, :, p * ocells:(p + 1) * ocells] = moved(field, sh, sw, oside).astype(bf16)
            for half in range(halves):
                block = jnp.concatenate([hall[p, d, :, half * size:(half + 1) * size] for d in range(planes)], axis=0)
                values = nn(block, dmat[...])
                values = jnp.where(values > 0, values, leak_slope * values).astype(bf16)
                for d in range(planes):
                    for k in range(4):
                        begin = p * ocells + half * part
                        awide[d * 4 + k, :, begin:begin + part] = values[d * ch:(d + 1) * ch, k * part:(k + 1) * part]
        for sd, sh, sw, pairs in combos():
            depth = (ns - sd) * ocells
            rows = jnp.concatenate([awide[k, :, :depth] for k, _ in pairs], axis=0)
            values = nt(rows, gwide[sh * 2 + sw, :, sd * ocells:]) * scales[1]
            for place, (_, k) in enumerate(pairs):
                f2_ref[k] = values[place * ch:(place + 1) * ch]
    sum1.second()

    weights = jnp.concatenate(
        [w1_ref[kd * nine:(kd + 1) * nine].reshape(nine * ch, all_ch) for kd in reversed(range(TAPS))], axis=1)
    for d in range(planes):
        stack = pbuf[d:d + TAPS].reshape(TAPS * all_ch, cells)
        out = nn(weights, stack)
        result = None
        for kh in range(TAPS):
            rows = None
            for kw in range(TAPS):
                k = kh * TAPS + kw
                term = moved(out[k * ch:(k + 1) * ch], 0, 1 - kw, side)
                rows = term if rows is None else rows + term
            rows = moved(rows, 1 - kh, 0, side)
            result = rows if result is None else result + rows
        in_ref[d] = result.astype(bf16)

    if not line:
        sum2.third()
    sum1.third()
    if not line:
        sum2.last()
        f2_ref[...] = o2[0:count].astype(f32)
    sum1.last()
    f1_ref[...] = o1[0:count].astype(f32)

    for item in g_copies + [p_spread, sum1] + ([] if line else [sum2]):
        item.wait_send()

    if line:
        for j in range(1, ns):
            maybe(has(j, False), others[j - 1].wait_send)
            maybe(has(j, True), wide[j - 1].wait_send)
        for j in range(ns - 1):
            pl.when((s >= j) & (s < ns - 1))(right[j].wait_send)
            pl.when((s <= ns - 1 - j) & (s > 0))(left[j].wait_send)

    @pl.when(below)
    def _():
        for item in n_copies + [d_copy, u_spread]:
            item.wait_send()

    @pl.when(above)
    def _():
        for item in [u_copy, d_spread]:
            item.wait_send()


def shards(nc, ns, inputs, pre_act, out_grad, weight_one, weight_two):
    samples, ch, planes, cells = inputs.shape
    goc, oplanes, ocells = out_grad.shape[1:]
    assert samples == 1 and planes == 2 and oplanes == 1
    side = math.isqrt(cells)
    count = TAPS ** 3
    x = jnp.swapaxes(inputs[0], 0, 1)
    h = jnp.swapaxes(pre_act[0], 0, 1)
    g = out_grad.reshape(goc, ocells)
    all_ch, all_goc = weight_one.shape[4], weight_two.shape[4]
    w1 = weight_one.reshape(count, ch, all_ch)
    w2 = weight_two.reshape(count, ch, all_goc)
    line = ns == LINE
    spread = count if line else -(-count // ns) * ns
    got = 2 * count if line else spread
    lanes = max(ns, CHUNKS)
    spread2, got2 = (1, 1) if line else (spread, got)
    every = ns if line else 1
    size = min(cells, 4 * 128)
    scales = (1.0 / math.sqrt(samples * planes * ns * cells), 1.0 / math.sqrt(samples * oplanes * ns * ocells))
    vmem = pl.BlockSpec(memory_space=pltpu.VMEM)
    dma = pltpu.SemaphoreType.DMA
    out, one, two = pl.pallas_call(
        functools.partial(kernel, nc, ns, side, scales),
        out_shape=(
            jax.ShapeDtypeStruct((planes, ch, cells), bf16),
            jax.ShapeDtypeStruct((count, ch, all_ch), f32),
            jax.ShapeDtypeStruct((count, ch, all_goc), f32),
        ),
        in_specs=[vmem] * 5,
        out_specs=(vmem,) * 3,
        scratch_shapes=[
            pltpu.VMEM((2, all_goc, ocells), bf16),
            pltpu.VMEM((8, all_goc, ocells), bf16),
            pltpu.VMEM((8, ch, ocells), f32),
            pltpu.VMEM((size, size), bf16),
            pltpu.VMEM((planes + 2, all_ch, cells), bf16),
            pltpu.VMEM((planes, TAPS * TAPS * ch, cells), bf16),
            pltpu.VMEM((spread, ch, all_ch), bf16),
            pltpu.VMEM((spread2, ch, all_goc), bf16),
            pltpu.VMEM((got, ch, all_ch), bf16),
            pltpu.VMEM((got2, ch, all_goc), bf16),
            pltpu.VMEM((spread, ch, all_ch), bf16),
            pltpu.VMEM((spread2, ch, all_goc), bf16),
            pltpu.VMEM((spread, ch, all_ch), bf16),
            pltpu.VMEM((spread2, ch, all_goc), bf16),
            dma((2, nc)), dma((2, nc)), dma((2, nc)), dma((2, nc)), dma((2, nc)),
            dma((2, lanes)), dma((2, lanes)), dma((2, lanes)), dma((2, lanes)), dma((2, lanes)), dma((2, lanes)),
            pltpu.VMEM((every, planes, ch, cells), bf16),
            pltpu.VMEM((every, all_goc, ocells), bf16),
            pltpu.VMEM((4, all_goc, every * ocells), bf16),
            pltpu.VMEM((8, ch, every * ocells), bf16),
            dma((2, every)), dma((2, every)), dma((2, every)), dma((2, every * nc)),
        ],
        compiler_params=pltpu.CompilerParams(
            collective_id=0, has_side_effects=True, vmem_limit_bytes=48 * 1024 * 1024),
    )(x, h, g, w1, w2)
    in_grad = jnp.swapaxes(out, 0, 1).reshape(inputs.shape)
    return (in_grad, one.reshape(TAPS, TAPS, TAPS, ch, all_ch), two.reshape(TAPS, TAPS, TAPS, ch, all_goc))


def solution(mesh):
    in_specs = (
        P("groups", "chan", "space", None),
        P("groups", "chan", "space", None),
        P("groups", "chan", "space", None),
        P(None, None, None, "chan", None),
        P(None, None, None, "chan", None),
    )
    out_specs = (
        P("groups", "chan", "space", None),
        P("groups", None, None, "chan", None),
        P("groups", None, None, "chan", None),
    )
    body = functools.partial(shards, mesh.shape["chan"], mesh.shape["space"])
    return jax.shard_map(body, mesh=mesh, in_specs=in_specs, out_specs=out_specs, check_vma=False)
```

```python
import functools
import math

import jax
import jax.numpy as jnp
from jax import lax
from jax.experimental import pallas as pl
from jax.experimental.pallas import tpu as pltpu
from jax.sharding import PartitionSpec as P

TAPS = 3
LINE = 4
CHUNKS = 9
LAG = 4
leak_slope = 0.3
MESH = pl.DeviceIdType.MESH
f32, bf16 = jnp.float32, jnp.bfloat16


def nt(a, b):
    return lax.dot_general(a, b, (((1,), (1,)), ((), ())), preferred_element_type=f32)


def nn(a, b):
    return jnp.dot(a, b, preferred_element_type=f32)


def lane_iota(shape):
    return lax.broadcasted_iota(jnp.int32, shape, 1)


def moved(value, row_step, col_step, side):
    length = value.shape[1]
    offset = row_step * side + col_step
    if offset % length:
        value = pltpu.roll(value, (-offset) % length, 1)
    lane = lane_iota((1, length))
    row, col = lane // side + row_step, lane % side + col_step
    if row_step or col_step:
        keep = (row >= 0) & (row < side) & (col >= 0) & (col < side)
        value = jnp.where(keep, value, 0.0)
    return value


def one_axis(shift):
    return [(0, 1), (1, 2)] if shift == 0 else [(1, 0)]


def combos():
    result = []
    for sd in range(2):
        for sh in range(2):
            for sw in range(2):
                pairs = []
                for d, kd in one_axis(sd):
                    for a, kh in one_axis(sh):
                        for b, kw in one_axis(sw):
                            pairs.append((d * 4 + a * 2 + b, (kd * TAPS + kh) * TAPS + kw))
                result.append((sd, sh, sw, pairs))
    return result


def kernel(nc, ns, side, scales, x_ref, h_ref, g_ref, w1_ref, w2_ref,
           in_ref, f1_ref, f2_ref,
           gbuf, gsh, hcls, dmat, pbuf, xs, s1, s2, r1, r2, o1, o2, b1, b2,
           g_sem, n_sem, p_sem, u_sem, d_sem, a1_sem, a2_sem, c1_sem, c2_sem, m1_sem, m2_sem,
           hall, gall, gwide, awide, r_sem, l_sem, o_sem, os_sem):
    s, c = lax.axis_index("space"), lax.axis_index("chan")
    planes, ch, cells = x_ref.shape
    goc = g_ref.shape[0]
    oside = side // 2
    ocells = g_ref.shape[1]
    count = w1_ref.shape[0]
    line = ns == LINE

    def at_chan(t):
        return lax.rem(c + t, nc)

    def at_space(t):
        return lax.rem(s + t, ns)

    offsets = {(i % ns, j) for i in (-1, 0, 1) for j in range(nc)}
    offsets |= {(i, 0) for i in range(ns)}
    offsets = sorted(offsets - {(0, 0)})
    barrier = pltpu.get_barrier_semaphore()
    for i, j in offsets:
        pl.semaphore_signal(barrier, inc=1, device_id={"space": at_space(i), "chan": at_chan(j)}, device_id_type=MESH)
    if line:
        hall[s] = h_ref[...]

    @pl.when(s == ns - 1)
    def _():
        gbuf[1] = jnp.zeros(gbuf.shape[1:], bf16)
        pbuf[planes + 1] = jnp.zeros(pbuf.shape[1:], bf16)

    @pl.when(s == 0)
    def _():
        pbuf[0] = jnp.zeros(pbuf.shape[1:], bf16)

    size = dmat.shape[0]
    part = size // 4
    halves = cells // size
    lane = lane_iota((1, size))
    cls, inner = lane // part, lane % part
    target = (2 * (inner // oside) + cls // 2) * side + 2 * (inner % oside) + cls % 2
    dmat[...] = jnp.where(lax.broadcasted_iota(jnp.int32, (size, size), 0) == target, 1.0, 0.0).astype(bf16)
    for half in range(halves):
        block = jnp.concatenate([h_ref[d, :, half * size:(half + 1) * size] for d in range(planes)], axis=0)
        found = nn(block, dmat[...])
        for d in range(planes):
            for k in range(4):
                hcls[d * 4 + k, :, half * part:(half + 1) * part] = found[d * ch:(d + 1) * ch, k * part:(k + 1) * part]

    for d in range(planes):
        field = x_ref[d].astype(f32)
        for kh in range(TAPS):
            for kw in range(TAPS):
                k = kh * TAPS + kw
                xs[d, k * ch:(k + 1) * ch, :] = moved(field, kh - 1, kw - 1, side).astype(bf16)

    pl.semaphore_wait(barrier, len(offsets))

    def remote(src, dst, sem, i, where):
        return pltpu.make_async_remote_copy(
            src_ref=src, dst_ref=dst, send_sem=sem.at[0, i], recv_sem=sem.at[1, i],
            device_id=where, device_id_type=MESH)

    class Spread:
        def __init__(self, field, where, rows, sem, base=0):
            def block(index):
                return field.at[where, pl.ds(pl.multiple_of(index * rows, rows), rows)]

            mine = block(c)
            if nc == 4:
                near, far = c + 1 - 2 * lax.rem(c, 2), lax.rem(c + 2, nc)
                self.far = remote(mine, mine, sem, base + 2, {"chan": far})
                self.near = remote(mine, mine, sem, base + 1, {"chan": near})
                self.onward = remote(block(far), block(far), sem, base + 3, {"chan": near})
                self.first, self.all = [self.far, self.near], [self.far, self.near, self.onward]
            else:
                self.onward = None
                self.first = self.all = [remote(mine, mine, sem, base + t, {"chan": at_chan(t)}) for t in range(1, nc)]

        def start(self):
            for copy in self.first:
                copy.start()

        def forward(self):
            if self.onward is not None:
                self.far.wait_recv()
                self.onward.start()

        def wait_recv(self):
            for copy in self.all if self.onward is None else [self.near, self.onward]:
                copy.wait_recv()

        def wait_send(self):
            for copy in self.all:
                copy.wait_send()

    g_rows = pl.ds(pl.multiple_of(c * goc, goc), goc)
    g_copies = [remote(g_ref, gbuf.at[0, g_rows], g_sem, t, {"chan": at_chan(t)}) for t in range(1, nc)]
    n_copies = [remote(g_ref, gbuf.at[1, g_rows], n_sem, t,
                       {"space": lax.max(s - 1, 0), "chan": at_chan(t)}) for t in range(nc)]
    for copy in g_copies:
        copy.start()

    @pl.when(s > 0)
    def _():
        for copy in n_copies:
            copy.start()

    gbuf[0, g_rows, :] = g_ref[...]

    if line:
        to_next, to_last = {"space": lax.min(s + 1, ns - 1)}, {"space": lax.max(s - 1, 0)}
        right, left = [], []
        for j in range(ns - 1):
            block = hall.at[lax.max(s - j, 0)]
            right.append(remote(h_ref if j == 0 else block, block, r_sem, j, to_next))
            block = hall.at[lax.min(s + j, ns - 1)]
            left.append(remote(h_ref if j == 0 else block, block, l_sem, j, to_last))
        others = [remote(g_ref, gall.at[s, g_rows], o_sem, j, {"space": at_space(ns - j)}) for j in range(1, ns)]

        def has(j, other):
            return None if j > 1 else (s == 0 if not other else s == ns - 1)

        def maybe(cond, run):
            if cond is None:
                run()
            else:
                pl.when(cond)(run)

        for j in range(1, ns):
            maybe(has(j, False), others[j - 1].start)

        def pass_on(j):
            @pl.when(s >= j)
            def _():
                right[j - 1].wait_recv()

            @pl.when(s <= ns - 1 - j)
            def _():
                left[j - 1].wait_recv()

            if j < ns - 1:
                pl.when((s >= j) & (s < ns - 1))(right[j].start)
                pl.when((s <= ns - 1 - j) & (s > 0))(left[j].start)

    for copy in g_copies:
        copy.wait_recv()
    for sd in range(2):
        if sd == 1:
            @pl.when(s < ns - 1)
            def _():
                for copy in n_copies:
                    copy.wait_recv()
        field = gbuf[sd].astype(f32)
        for sh in range(2):
            for sw in range(2):
                gsh[sd * 4 + sh * 2 + sw] = moved(field, sh, sw, oside).astype(bf16)

    if line:
        pl.when(s < ns - 1)(right[0].start)
        pl.when(s > 0)(left[0].start)

    total = [None] * 8
    for index, (_, _, _, pairs) in enumerate(combos()):
        weights = jnp.concatenate([w2_ref[k] for _, k in pairs], axis=0)
        found = nn(weights, gsh[index])
        for place, (k, _) in enumerate(pairs):
            piece = found[place * ch:(place + 1) * ch]
            total[k] = piece if total[k] is None else total[k] + piece
    grads = [jnp.where(hcls[k] > 0, total[k], leak_slope * total[k]).astype(bf16) for k in range(8)]

    def rows_of(index):
        return pl.ds(pl.multiple_of(index * ch, ch), ch)

    p_rows = rows_of(c)
    for half in range(halves):
        block = jnp.concatenate([
            jnp.concatenate([grads[d * 4 + k][:, half * part:(half + 1) * part] for k in range(4)], axis=1)
            for d in range(planes)], axis=0)
        found = nt(block, dmat[...]).astype(bf16)
        for d in range(planes):
            pbuf[1 + d, p_rows, half * size:(half + 1) * size] = found[d * ch:(d + 1) * ch]

    u_copy = remote(pbuf.at[planes, p_rows], pbuf.at[0, p_rows], u_sem, 0, {"space": lax.min(s + 1, ns - 1)})
    d_copy = remote(pbuf.at[1, p_rows], pbuf.at[planes + 1, p_rows], d_sem, 0, {"space": lax.max(s - 1, 0)})

    p_spread = Spread(pbuf, pl.ds(1, planes), ch, p_sem)
    u_spread = Spread(pbuf, 0, ch, u_sem)
    d_spread = Spread(pbuf, planes + 1, ch, d_sem)
    below, above = s > 0, s < ns - 1

    pl.when(above)(u_copy.start)
    pl.when(below)(d_copy.start)
    p_spread.start()

    if line:
        wide = [Spread(gall, lax.rem(s + j, ns), goc, os_sem, j * nc) for j in range(1, ns)]
        gall[s] = gbuf[0]

        @pl.when(s < ns - 1)
        def _():
            gall[lax.min(s + 1, ns - 1)] = gbuf[1]

    if not line:
        act = [jnp.where(hcls[k] > 0, hcls[k], leak_slope * hcls[k]).astype(bf16) for k in range(8)]
        for index, (_, _, _, pairs) in enumerate(combos()):
            found = nt(jnp.concatenate([act[k] for k, _ in pairs], axis=0), gsh[index])
            for place, (_, k) in enumerate(pairs):
                s2[k] = found[place * ch:(place + 1) * ch].astype(bf16)
    for k in range(count, s1.shape[0]):
        if not line:
            s2[k] = jnp.zeros(s2.shape[1:], bf16)
        s1[k] = jnp.zeros(s1.shape[1:], bf16)

    step = -(-count // (CHUNKS if line else ns))
    pieces = [(i, min(step, count - i)) for i in range(0, count, step)]

    class Sum:
        def __init__(self, src, got, mid, out, scale, sems):
            self.src, self.got, self.mid, self.out, self.scale = src, got, mid, out, scale
            self.sems = sems
            if line:
                inner, end, mate = 1 + s // (ns - 1), (ns - 1) * (s // 2), ns - 1 - s
                self.up, self.across, self.down = [], [], []
                for k, (i, n) in enumerate(pieces):
                    part, later = pl.ds(i, n), pl.ds(count + i, n)
                    self.up.append(remote(src.at[part], got.at[part], sems[0], k, {"space": inner}))
                    self.across.append(remote(mid.at[part], got.at[later], sems[1], k, {"space": mate}))
                    self.down.append(remote(out.at[part], out.at[part], sems[2], k, {"space": end}))
            else:
                own = pl.ds(s * step, step)
                self.scatters = [remote(src.at[pl.ds(at_space(t) * step, step)], got.at[pl.ds(t * step, step)],
                                        sems[0], t, {"space": at_space(t)}) for t in range(1, ns)]
                self.gathers = [remote(out.at[own], out.at[own], sems[2], t, {"space": at_space(t)})
                                for t in range(1, ns)]

        def first(self):
            if line:
                @pl.when(outer)
                def _():
                    for copy in self.up:
                        copy.start()
            else:
                for copy in self.scatters:
                    copy.start()

        def third(self):
            if line:
                def over(k):
                    (i, n), up, across = pieces[k], self.up[k], self.across[k]
                    up.wait_recv()
                    value = self.src[i:i + n].astype(f32) + self.got[i:i + n].astype(f32)
                    self.mid[i:i + n] = value.astype(bf16)
                    across.start()

                def back(k):
                    (i, n), across, down = pieces[k], self.across[k], self.down[k]
                    across.wait_recv()
                    value = self.mid[i:i + n].astype(f32) + self.got[count + i:count + i + n].astype(f32)
                    self.out[i:i + n] = (value * self.scale).astype(bf16)
                    down.start()

                @pl.when(jnp.logical_not(outer))
                def _():
                    for k in range(len(pieces) + LAG):
                        if k < len(pieces):
                            over(k)
                        if k >= LAG:
                            back(k - LAG)
            else:
                own = pl.ds(s * step, step)
                value = self.src[own].astype(f32)
                for t, copy in enumerate(self.scatters, 1):
                    copy.wait_recv()
                    value = value + self.got[t * step:(t + 1) * step].astype(f32)
                self.out[own] = (value * self.scale).astype(bf16)
                for copy in self.gathers:
                    copy.start()

        def last(self):
            if line:
                @pl.when(outer)
                def _():
                    for copy in self.down:
                        copy.wait_recv()
            else:
                for copy in self.gathers:
                    copy.wait_recv()

        def wait_send(self):
            if line:
                @pl.when(outer)
                def _():
                    for copy in self.up:
                        copy.wait_send()

                @pl.when(jnp.logical_not(outer))
                def _():
                    for copy in self.across + self.down:
                        copy.wait_send()
            else:
                for copy in self.scatters + self.gathers:
                    copy.wait_send()

    outer = (s == 0) | (s == ns - 1)
    sum2 = None if line else Sum(s2, r2, b2, o2, scales[1], (a2_sem, m2_sem, c2_sem))
    sum1 = Sum(s1, r1, b1, o1, scales[0], (a1_sem, m1_sem, c1_sem))
    if not line:
        sum2.first()

    @pl.when(below)
    def _():
        u_copy.wait_recv()
        u_spread.start()

    @pl.when(above)
    def _():
        d_copy.wait_recv()
        d_spread.start()

    if line:
        pass_on(1)
    p_spread.forward()

    @pl.when(below)
    def _():
        u_spread.forward()

    @pl.when(above)
    def _():
        d_spread.forward()

    if line:
        pass_on(2)
    p_spread.wait_recv()

    @pl.when(below)
    def _():
        u_spread.wait_recv()

    @pl.when(above)
    def _():
        d_spread.wait_recv()

    if line:
        for j in range(1, ns):
            def relay(j=j):
                others[j - 1].wait_recv()
                wide[j - 1].start()

            maybe(has(j, True), relay)

    all_ch = pbuf.shape[1]
    found = None
    for d in range(planes):
        stack = pbuf[d:d + TAPS].reshape(TAPS * all_ch, cells)
        term = nt(xs[d], stack)
        found = term if found is None else found + term
    nine = TAPS * TAPS
    for kd in range(TAPS):
        column = (TAPS - 1 - kd) * all_ch
        for k in range(nine):
            s1[kd * nine + k] = found[k * ch:(k + 1) * ch, column:column + all_ch].astype(bf16)
    sum1.first()


    weights = jnp.concatenate(
        [w1_ref[kd * nine:(kd + 1) * nine].reshape(nine * ch, all_ch) for kd in reversed(range(TAPS))], axis=1)
    for d in range(planes):
        stack = pbuf[d:d + TAPS].reshape(TAPS * all_ch, cells)
        out = nn(weights, stack)
        result = None
        for kh in range(TAPS):
            rows = None
            for kw in range(TAPS):
                k = kh * TAPS + kw
                term = moved(out[k * ch:(k + 1) * ch], 0, 1 - kw, side)
                rows = term if rows is None else rows + term
            rows = moved(rows, 1 - kh, 0, side)
            result = rows if result is None else result + rows
        in_ref[d] = result.astype(bf16)

    if line:
        for j in range(1, ns):
            maybe(has(j, True), wide[j - 1].forward)
    else:
        sum2.third()
    sum1.third()

    if line:
        pass_on(ns - 1)
        for j in range(1, ns):
            maybe(has(j, True), wide[j - 1].wait_recv)
        for p in range(ns):
            field = gall[p].astype(f32)
            for sh in range(2):
                for sw in range(2):
                    gwide[sh * 2 + sw, :, p * ocells:(p + 1) * ocells] = moved(field, sh, sw, oside).astype(bf16)
            for half in range(halves):
                block = jnp.concatenate([hall[p, d, :, half * size:(half + 1) * size] for d in range(planes)], axis=0)
                values = nn(block, dmat[...])
                values = jnp.where(values > 0, values, leak_slope * values).astype(bf16)
                for d in range(planes):
                    for k in range(4):
                        begin = p * ocells + half * part
                        awide[d * 4 + k, :, begin:begin + part] = values[d * ch:(d + 1) * ch, k * part:(k + 1) * part]
        for sd, sh, sw, pairs in combos():
            depth = (ns - sd) * ocells
            rows = jnp.concatenate([awide[k, :, :depth] for k, _ in pairs], axis=0)
            values = nt(rows, gwide[sh * 2 + sw, :, sd * ocells:]) * scales[1]
            for place, (_, k) in enumerate(pairs):
                f2_ref[k] = values[place * ch:(place + 1) * ch]
    if not line:
        sum2.last()
        f2_ref[...] = o2[0:count].astype(f32)
    sum1.last()
    f1_ref[...] = o1[0:count].astype(f32)

    for item in g_copies + [p_spread, sum1] + ([] if line else [sum2]):
        item.wait_send()

    if line:
        for j in range(1, ns):
            maybe(has(j, False), others[j - 1].wait_send)
            maybe(has(j, True), wide[j - 1].wait_send)
        for j in range(ns - 1):
            pl.when((s >= j) & (s < ns - 1))(right[j].wait_send)
            pl.when((s <= ns - 1 - j) & (s > 0))(left[j].wait_send)

    @pl.when(below)
    def _():
        for item in n_copies + [d_copy, u_spread]:
            item.wait_send()

    @pl.when(above)
    def _():
        for item in [u_copy, d_spread]:
            item.wait_send()


def shards(nc, ns, inputs, pre_act, out_grad, weight_one, weight_two):
    samples, ch, planes, cells = inputs.shape
    goc, oplanes, ocells = out_grad.shape[1:]
    assert samples == 1 and planes == 2 and oplanes == 1
    side = math.isqrt(cells)
    count = TAPS ** 3
    x = jnp.swapaxes(inputs[0], 0, 1)
    h = jnp.swapaxes(pre_act[0], 0, 1)
    g = out_grad.reshape(goc, ocells)
    all_ch, all_goc = weight_one.shape[4], weight_two.shape[4]
    w1 = weight_one.reshape(count, ch, all_ch)
    w2 = weight_two.reshape(count, ch, all_goc)
    line = ns == LINE
    spread = count if line else -(-count // ns) * ns
    got = 2 * count if line else spread
    lanes = max(ns, CHUNKS)
    spread2, got2 = (1, 1) if line else (spread, got)
    every = ns if line else 1
    size = min(cells, 4 * 128)
    scales = (1.0 / math.sqrt(samples * planes * ns * cells), 1.0 / math.sqrt(samples * oplanes * ns * ocells))
    vmem = pl.BlockSpec(memory_space=pltpu.VMEM)
    dma = pltpu.SemaphoreType.DMA
    out, one, two = pl.pallas_call(
        functools.partial(kernel, nc, ns, side, scales),
        out_shape=(
            jax.ShapeDtypeStruct((planes, ch, cells), bf16),
            jax.ShapeDtypeStruct((count, ch, all_ch), f32),
            jax.ShapeDtypeStruct((count, ch, all_goc), f32),
        ),
        in_specs=[vmem] * 5,
        out_specs=(vmem,) * 3,
        scratch_shapes=[
            pltpu.VMEM((2, all_goc, ocells), bf16),
            pltpu.VMEM((8, all_goc, ocells), bf16),
            pltpu.VMEM((8, ch, ocells), f32),
            pltpu.VMEM((size, size), bf16),
            pltpu.VMEM((planes + 2, all_ch, cells), bf16),
            pltpu.VMEM((planes, TAPS * TAPS * ch, cells), bf16),
            pltpu.VMEM((spread, ch, all_ch), bf16),
            pltpu.VMEM((spread2, ch, all_goc), bf16),
            pltpu.VMEM((got, ch, all_ch), bf16),
            pltpu.VMEM((got2, ch, all_goc), bf16),
            pltpu.VMEM((spread, ch, all_ch), bf16),
            pltpu.VMEM((spread2, ch, all_goc), bf16),
            pltpu.VMEM((spread, ch, all_ch), bf16),
            pltpu.VMEM((spread2, ch, all_goc), bf16),
            dma((2, nc)), dma((2, nc)), dma((2, nc)), dma((2, nc)), dma((2, nc)),
            dma((2, lanes)), dma((2, lanes)), dma((2, lanes)), dma((2, lanes)), dma((2, lanes)), dma((2, lanes)),
            pltpu.VMEM((every, planes, ch, cells), bf16),
            pltpu.VMEM((every, all_goc, ocells), bf16),
            pltpu.VMEM((4, all_goc, every * ocells), bf16),
            pltpu.VMEM((8, ch, every * ocells), bf16),
            dma((2, every)), dma((2, every)), dma((2, every)), dma((2, every * nc)),
        ],
        compiler_params=pltpu.CompilerParams(
            collective_id=0, has_side_effects=True, vmem_limit_bytes=48 * 1024 * 1024),
    )(x, h, g, w1, w2)
    in_grad = jnp.swapaxes(out, 0, 1).reshape(inputs.shape)
    return (in_grad, one.reshape(TAPS, TAPS, TAPS, ch, all_ch), two.reshape(TAPS, TAPS, TAPS, ch, all_goc))


def solution(mesh):
    in_specs = (
        P("groups", "chan", "space", None),
        P("groups", "chan", "space", None),
        P("groups", "chan", "space", None),
        P(None, None, None, "chan", None),
        P(None, None, None, "chan", None),
    )
    out_specs = (
        P("groups", "chan", "space", None),
        P("groups", None, None, "chan", None),
        P("groups", None, None, "chan", None),
    )
    body = functools.partial(shards, mesh.shape["chan"], mesh.shape["space"])
    return jax.shard_map(body, mesh=mesh, in_specs=in_specs, out_specs=out_specs, check_vma=False)
```

```python
import functools
import math

import jax
import jax.numpy as jnp
from jax import lax
from jax.experimental import pallas as pl
from jax.experimental.pallas import tpu as pltpu
from jax.sharding import PartitionSpec as P

TAPS = 3
LINE = 4
CHUNKS = 9
LAG = 4
leak_slope = 0.3
MESH = pl.DeviceIdType.MESH
f32, bf16 = jnp.float32, jnp.bfloat16


def nt(a, b):
    return lax.dot_general(a, b, (((1,), (1,)), ((), ())), preferred_element_type=f32)


def nn(a, b):
    return jnp.dot(a, b, preferred_element_type=f32)


def lane_iota(shape):
    return lax.broadcasted_iota(jnp.int32, shape, 1)


def moved(value, row_step, col_step, side):
    length = value.shape[1]
    offset = row_step * side + col_step
    if offset % length:
        value = pltpu.roll(value, (-offset) % length, 1)
    lane = lane_iota((1, length))
    row, col = lane // side + row_step, lane % side + col_step
    if row_step or col_step:
        keep = (row >= 0) & (row < side) & (col >= 0) & (col < side)
        value = jnp.where(keep, value, 0.0)
    return value


def one_axis(shift):
    return [(0, 1), (1, 2)] if shift == 0 else [(1, 0)]


def combos():
    result = []
    for sd in range(2):
        for sh in range(2):
            for sw in range(2):
                pairs = []
                for d, kd in one_axis(sd):
                    for a, kh in one_axis(sh):
                        for b, kw in one_axis(sw):
                            pairs.append((d * 4 + a * 2 + b, (kd * TAPS + kh) * TAPS + kw))
                result.append((sd, sh, sw, pairs))
    return result


def kernel(nc, ns, side, scales, x_ref, h_ref, g_ref, w1_ref, w2_ref,
           in_ref, f1_ref, f2_ref,
           gbuf, gsh, hcls, dmat, pbuf, xs, s1, s2, r1, r2, o1, o2, b1, b2,
           g_sem, n_sem, p_sem, u_sem, d_sem, a1_sem, a2_sem, c1_sem, c2_sem, m1_sem, m2_sem,
           hall, gall, gwide, awide, r_sem, l_sem, o_sem, os_sem):
    s, c = lax.axis_index("space"), lax.axis_index("chan")
    planes, ch, cells = x_ref.shape
    goc = g_ref.shape[0]
    oside = side // 2
    ocells = g_ref.shape[1]
    count = w1_ref.shape[0]
    line = ns == LINE

    def at_chan(t):
        return lax.rem(c + t, nc)

    def at_space(t):
        return lax.rem(s + t, ns)

    offsets = {(i % ns, j) for i in (-1, 0, 1) for j in range(nc)}
    offsets |= {(i, 0) for i in range(ns)}
    offsets = sorted(offsets - {(0, 0)})
    barrier = pltpu.get_barrier_semaphore()
    for i, j in offsets:
        pl.semaphore_signal(barrier, inc=1, device_id={"space": at_space(i), "chan": at_chan(j)}, device_id_type=MESH)
    if line:
        hall[s] = h_ref[...]

    @pl.when(s == ns - 1)
    def _():
        gbuf[1] = jnp.zeros(gbuf.shape[1:], bf16)
        pbuf[planes + 1] = jnp.zeros(pbuf.shape[1:], bf16)

    @pl.when(s == 0)
    def _():
        pbuf[0] = jnp.zeros(pbuf.shape[1:], bf16)

    size = dmat.shape[0]
    part = size // 4
    halves = cells // size
    lane = lane_iota((1, size))
    cls, inner = lane // part, lane % part
    target = (2 * (inner // oside) + cls // 2) * side + 2 * (inner % oside) + cls % 2
    dmat[...] = jnp.where(lax.broadcasted_iota(jnp.int32, (size, size), 0) == target, 1.0, 0.0).astype(bf16)
    for half in range(halves):
        block = jnp.concatenate([h_ref[d, :, half * size:(half + 1) * size] for d in range(planes)], axis=0)
        found = nn(block, dmat[...])
        for d in range(planes):
            for k in range(4):
                hcls[d * 4 + k, :, half * part:(half + 1) * part] = found[d * ch:(d + 1) * ch, k * part:(k + 1) * part]

    for d in range(planes):
        field = x_ref[d].astype(f32)
        for kh in range(TAPS):
            for kw in range(TAPS):
                k = kh * TAPS + kw
                xs[d, k * ch:(k + 1) * ch, :] = moved(field, kh - 1, kw - 1, side).astype(bf16)

    pl.semaphore_wait(barrier, len(offsets))

    def remote(src, dst, sem, i, where):
        return pltpu.make_async_remote_copy(
            src_ref=src, dst_ref=dst, send_sem=sem.at[0, i], recv_sem=sem.at[1, i],
            device_id=where, device_id_type=MESH)

    class Spread:
        def __init__(self, field, where, rows, sem, base=0):
            def block(index):
                return field.at[where, pl.ds(pl.multiple_of(index * rows, rows), rows)]

            mine = block(c)
            if nc == 4:
                near, far = c + 1 - 2 * lax.rem(c, 2), lax.rem(c + 2, nc)
                self.far = remote(mine, mine, sem, base + 2, {"chan": far})
                self.near = remote(mine, mine, sem, base + 1, {"chan": near})
                self.onward = remote(block(far), block(far), sem, base + 3, {"chan": near})
                self.first, self.all = [self.far, self.near], [self.far, self.near, self.onward]
            else:
                self.onward = None
                self.first = self.all = [remote(mine, mine, sem, base + t, {"chan": at_chan(t)}) for t in range(1, nc)]

        def start(self):
            for copy in self.first:
                copy.start()

        def forward(self):
            if self.onward is not None:
                self.far.wait_recv()
                self.onward.start()

        def wait_recv(self):
            for copy in self.all if self.onward is None else [self.near, self.onward]:
                copy.wait_recv()

        def wait_send(self):
            for copy in self.all:
                copy.wait_send()

    g_rows = pl.ds(pl.multiple_of(c * goc, goc), goc)
    g_copies = [remote(g_ref, gbuf.at[0, g_rows], g_sem, t, {"chan": at_chan(t)}) for t in range(1, nc)]
    n_copies = [remote(g_ref, gbuf.at[1, g_rows], n_sem, t,
                       {"space": lax.max(s - 1, 0), "chan": at_chan(t)}) for t in range(nc)]
    for copy in g_copies:
        copy.start()

    @pl.when(s > 0)
    def _():
        for copy in n_copies:
            copy.start()

    gbuf[0, g_rows, :] = g_ref[...]

    if line:
        to_next, to_last = {"space": lax.min(s + 1, ns - 1)}, {"space": lax.max(s - 1, 0)}
        right, left = [], []
        for j in range(ns - 1):
            block = hall.at[lax.max(s - j, 0)]
            right.append(remote(h_ref if j == 0 else block, block, r_sem, j, to_next))
            block = hall.at[lax.min(s + j, ns - 1)]
            left.append(remote(h_ref if j == 0 else block, block, l_sem, j, to_last))
        others = [remote(g_ref, gall.at[s, g_rows], o_sem, j, {"space": at_space(ns - j)}) for j in range(1, ns)]

        def has(j, other):
            return None if j > 1 else (s == 0 if not other else s == ns - 1)

        def maybe(cond, run):
            if cond is None:
                run()
            else:
                pl.when(cond)(run)

        for j in range(1, ns):
            maybe(has(j, False), others[j - 1].start)
        pl.when(s < ns - 1)(right[0].start)
        pl.when(s > 0)(left[0].start)

        def pass_on(j):
            @pl.when(s >= j)
            def _():
                right[j - 1].wait_recv()

            @pl.when(s <= ns - 1 - j)
            def _():
                left[j - 1].wait_recv()

            if j < ns - 1:
                pl.when((s >= j) & (s < ns - 1))(right[j].start)
                pl.when((s <= ns - 1 - j) & (s > 0))(left[j].start)

    for copy in g_copies:
        copy.wait_recv()
    for sd in range(2):
        if sd == 1:
            @pl.when(s < ns - 1)
            def _():
                for copy in n_copies:
                    copy.wait_recv()
        field = gbuf[sd].astype(f32)
        for sh in range(2):
            for sw in range(2):
                gsh[sd * 4 + sh * 2 + sw] = moved(field, sh, sw, oside).astype(bf16)

    total = [None] * 8
    for index, (_, _, _, pairs) in enumerate(combos()):
        weights = jnp.concatenate([w2_ref[k] for _, k in pairs], axis=0)
        found = nn(weights, gsh[index])
        for place, (k, _) in enumerate(pairs):
            piece = found[place * ch:(place + 1) * ch]
            total[k] = piece if total[k] is None else total[k] + piece
    grads = [jnp.where(hcls[k] > 0, total[k], leak_slope * total[k]).astype(bf16) for k in range(8)]

    def rows_of(index):
        return pl.ds(pl.multiple_of(index * ch, ch), ch)

    p_rows = rows_of(c)
    for half in range(halves):
        block = jnp.concatenate([
            jnp.concatenate([grads[d * 4 + k][:, half * part:(half + 1) * part] for k in range(4)], axis=1)
            for d in range(planes)], axis=0)
        found = nt(block, dmat[...]).astype(bf16)
        for d in range(planes):
            pbuf[1 + d, p_rows, half * size:(half + 1) * size] = found[d * ch:(d + 1) * ch]

    u_copy = remote(pbuf.at[planes, p_rows], pbuf.at[0, p_rows], u_sem, 0, {"space": lax.min(s + 1, ns - 1)})
    d_copy = remote(pbuf.at[1, p_rows], pbuf.at[planes + 1, p_rows], d_sem, 0, {"space": lax.max(s - 1, 0)})

    p_spread = Spread(pbuf, pl.ds(1, planes), ch, p_sem)
    u_spread = Spread(pbuf, 0, ch, u_sem)
    d_spread = Spread(pbuf, planes + 1, ch, d_sem)
    below, above = s > 0, s < ns - 1

    pl.when(above)(u_copy.start)
    pl.when(below)(d_copy.start)
    p_spread.start()

    if line:
        wide = [Spread(gall, lax.rem(s + j, ns), goc, os_sem, j * nc) for j in range(1, ns)]
        gall[s] = gbuf[0]

        @pl.when(s < ns - 1)
        def _():
            gall[lax.min(s + 1, ns - 1)] = gbuf[1]

    if not line:
        act = [jnp.where(hcls[k] > 0, hcls[k], leak_slope * hcls[k]).astype(bf16) for k in range(8)]
        for index, (_, _, _, pairs) in enumerate(combos()):
            found = nt(jnp.concatenate([act[k] for k, _ in pairs], axis=0), gsh[index])
            for place, (_, k) in enumerate(pairs):
                s2[k] = found[place * ch:(place + 1) * ch].astype(bf16)
    for k in range(count, s1.shape[0]):
        if not line:
            s2[k] = jnp.zeros(s2.shape[1:], bf16)
        s1[k] = jnp.zeros(s1.shape[1:], bf16)

    step = -(-count // (CHUNKS if line else ns))
    pieces = [(i, min(step, count - i)) for i in range(0, count, step)]

    class Sum:
        def __init__(self, src, got, mid, out, scale, sems):
            self.src, self.got, self.mid, self.out, self.scale = src, got, mid, out, scale
            self.sems = sems
            if line:
                inner, end, mate = 1 + s // (ns - 1), (ns - 1) * (s // 2), ns - 1 - s
                self.up, self.across, self.down = [], [], []
                for k, (i, n) in enumerate(pieces):
                    part, later = pl.ds(i, n), pl.ds(count + i, n)
                    self.up.append(remote(src.at[part], got.at[part], sems[0], k, {"space": inner}))
                    self.across.append(remote(mid.at[part], got.at[later], sems[1], k, {"space": mate}))
                    self.down.append(remote(out.at[part], out.at[part], sems[2], k, {"space": end}))
            else:
                own = pl.ds(s * step, step)
                self.scatters = [remote(src.at[pl.ds(at_space(t) * step, step)], got.at[pl.ds(t * step, step)],
                                        sems[0], t, {"space": at_space(t)}) for t in range(1, ns)]
                self.gathers = [remote(out.at[own], out.at[own], sems[2], t, {"space": at_space(t)})
                                for t in range(1, ns)]

        def first(self):
            if line:
                @pl.when(outer)
                def _():
                    for copy in self.up:
                        copy.start()
            else:
                for copy in self.scatters:
                    copy.start()

        def third(self):
            if line:
                def over(k):
                    (i, n), up, across = pieces[k], self.up[k], self.across[k]
                    up.wait_recv()
                    value = self.src[i:i + n].astype(f32) + self.got[i:i + n].astype(f32)
                    self.mid[i:i + n] = value.astype(bf16)
                    across.start()

                def back(k):
                    (i, n), across, down = pieces[k], self.across[k], self.down[k]
                    across.wait_recv()
                    value = self.mid[i:i + n].astype(f32) + self.got[count + i:count + i + n].astype(f32)
                    self.out[i:i + n] = (value * self.scale).astype(bf16)
                    down.start()

                @pl.when(jnp.logical_not(outer))
                def _():
                    for k in range(len(pieces) + LAG):
                        if k < len(pieces):
                            over(k)
                        if k >= LAG:
                            back(k - LAG)
            else:
                own = pl.ds(s * step, step)
                value = self.src[own].astype(f32)
                for t, copy in enumerate(self.scatters, 1):
                    copy.wait_recv()
                    value = value + self.got[t * step:(t + 1) * step].astype(f32)
                self.out[own] = (value * self.scale).astype(bf16)
                for copy in self.gathers:
                    copy.start()

        def last(self):
            if line:
                @pl.when(outer)
                def _():
                    for copy in self.down:
                        copy.wait_recv()
            else:
                for copy in self.gathers:
                    copy.wait_recv()

        def wait_send(self):
            if line:
                @pl.when(outer)
                def _():
                    for copy in self.up:
                        copy.wait_send()

                @pl.when(jnp.logical_not(outer))
                def _():
                    for copy in self.across + self.down:
                        copy.wait_send()
            else:
                for copy in self.scatters + self.gathers:
                    copy.wait_send()

    outer = (s == 0) | (s == ns - 1)
    sum2 = None if line else Sum(s2, r2, b2, o2, scales[1], (a2_sem, m2_sem, c2_sem))
    sum1 = Sum(s1, r1, b1, o1, scales[0], (a1_sem, m1_sem, c1_sem))
    if line:
        pass_on(1)
    else:
        sum2.first()

    @pl.when(below)
    def _():
        u_copy.wait_recv()
        u_spread.start()

    @pl.when(above)
    def _():
        d_copy.wait_recv()
        d_spread.start()

    p_spread.forward()

    @pl.when(below)
    def _():
        u_spread.forward()

    @pl.when(above)
    def _():
        d_spread.forward()

    if line:
        pass_on(2)
    p_spread.wait_recv()

    @pl.when(below)
    def _():
        u_spread.wait_recv()

    @pl.when(above)
    def _():
        d_spread.wait_recv()

    if line:
        for j in range(1, ns):
            def relay(j=j):
                others[j - 1].wait_recv()
                wide[j - 1].start()

            maybe(has(j, True), relay)

    all_ch = pbuf.shape[1]
    found = None
    for d in range(planes):
        stack = pbuf[d:d + TAPS].reshape(TAPS * all_ch, cells)
        term = nt(xs[d], stack)
        found = term if found is None else found + term
    nine = TAPS * TAPS
    for kd in range(TAPS):
        column = (TAPS - 1 - kd) * all_ch
        for k in range(nine):
            s1[kd * nine + k] = found[k * ch:(k + 1) * ch, column:column + all_ch].astype(bf16)
    sum1.first()


    weights = jnp.concatenate(
        [w1_ref[kd * nine:(kd + 1) * nine].reshape(nine * ch, all_ch) for kd in reversed(range(TAPS))], axis=1)
    for d in range(planes):
        stack = pbuf[d:d + TAPS].reshape(TAPS * all_ch, cells)
        out = nn(weights, stack)
        result = None
        for kh in range(TAPS):
            rows = None
            for kw in range(TAPS):
                k = kh * TAPS + kw
                term = moved(out[k * ch:(k + 1) * ch], 0, 1 - kw, side)
                rows = term if rows is None else rows + term
            rows = moved(rows, 1 - kh, 0, side)
            result = rows if result is None else result + rows
        in_ref[d] = result.astype(bf16)

    if line:
        for j in range(1, ns):
            maybe(has(j, True), wide[j - 1].forward)
    else:
        sum2.third()
    sum1.third()

    if line:
        pass_on(ns - 1)
        for j in range(1, ns):
            maybe(has(j, True), wide[j - 1].wait_recv)
        for p in range(ns):
            field = gall[p].astype(f32)
            for sh in range(2):
                for sw in range(2):
                    gwide[sh * 2 + sw, :, p * ocells:(p + 1) * ocells] = moved(field, sh, sw, oside).astype(bf16)
            for half in range(halves):
                block = jnp.concatenate([hall[p, d, :, half * size:(half + 1) * size] for d in range(planes)], axis=0)
                values = nn(block, dmat[...])
                values = jnp.where(values > 0, values, leak_slope * values).astype(bf16)
                for d in range(planes):
                    for k in range(4):
                        begin = p * ocells + half * part
                        awide[d * 4 + k, :, begin:begin + part] = values[d * ch:(d + 1) * ch, k * part:(k + 1) * part]
        for sd, sh, sw, pairs in combos():
            depth = (ns - sd) * ocells
            rows = jnp.concatenate([awide[k, :, :depth] for k, _ in pairs], axis=0)
            values = nt(rows, gwide[sh * 2 + sw, :, sd * ocells:]) * scales[1]
            for place, (_, k) in enumerate(pairs):
                f2_ref[k] = values[place * ch:(place + 1) * ch]
    if not line:
        sum2.last()
        f2_ref[...] = o2[0:count].astype(f32)
    sum1.last()
    f1_ref[...] = o1[0:count].astype(f32)

    for item in g_copies + [p_spread, sum1] + ([] if line else [sum2]):
        item.wait_send()

    if line:
        for j in range(1, ns):
            maybe(has(j, False), others[j - 1].wait_send)
            maybe(has(j, True), wide[j - 1].wait_send)
        for j in range(ns - 1):
            pl.when((s >= j) & (s < ns - 1))(right[j].wait_send)
            pl.when((s <= ns - 1 - j) & (s > 0))(left[j].wait_send)

    @pl.when(below)
    def _():
        for item in n_copies + [d_copy, u_spread]:
            item.wait_send()

    @pl.when(above)
    def _():
        for item in [u_copy, d_spread]:
            item.wait_send()


def shards(nc, ns, inputs, pre_act, out_grad, weight_one, weight_two):
    samples, ch, planes, cells = inputs.shape
    goc, oplanes, ocells = out_grad.shape[1:]
    assert samples == 1 and planes == 2 and oplanes == 1
    side = math.isqrt(cells)
    count = TAPS ** 3
    x = jnp.swapaxes(inputs[0], 0, 1)
    h = jnp.swapaxes(pre_act[0], 0, 1)
    g = out_grad.reshape(goc, ocells)
    all_ch, all_goc = weight_one.shape[4], weight_two.shape[4]
    w1 = weight_one.reshape(count, ch, all_ch)
    w2 = weight_two.reshape(count, ch, all_goc)
    line = ns == LINE
    spread = count if line else -(-count // ns) * ns
    got = 2 * count if line else spread
    lanes = max(ns, CHUNKS)
    spread2, got2 = (1, 1) if line else (spread, got)
    every = ns if line else 1
    size = min(cells, 4 * 128)
    scales = (1.0 / math.sqrt(samples * planes * ns * cells), 1.0 / math.sqrt(samples * oplanes * ns * ocells))
    vmem = pl.BlockSpec(memory_space=pltpu.VMEM)
    dma = pltpu.SemaphoreType.DMA
    out, one, two = pl.pallas_call(
        functools.partial(kernel, nc, ns, side, scales),
        out_shape=(
            jax.ShapeDtypeStruct((planes, ch, cells), bf16),
            jax.ShapeDtypeStruct((count, ch, all_ch), f32),
            jax.ShapeDtypeStruct((count, ch, all_goc), f32),
        ),
        in_specs=[vmem] * 5,
        out_specs=(vmem,) * 3,
        scratch_shapes=[
            pltpu.VMEM((2, all_goc, ocells), bf16),
            pltpu.VMEM((8, all_goc, ocells), bf16),
            pltpu.VMEM((8, ch, ocells), f32),
            pltpu.VMEM((size, size), bf16),
            pltpu.VMEM((planes + 2, all_ch, cells), bf16),
            pltpu.VMEM((planes, TAPS * TAPS * ch, cells), bf16),
            pltpu.VMEM((spread, ch, all_ch), bf16),
            pltpu.VMEM((spread2, ch, all_goc), bf16),
            pltpu.VMEM((got, ch, all_ch), bf16),
            pltpu.VMEM((got2, ch, all_goc), bf16),
            pltpu.VMEM((spread, ch, all_ch), bf16),
            pltpu.VMEM((spread2, ch, all_goc), bf16),
            pltpu.VMEM((spread, ch, all_ch), bf16),
            pltpu.VMEM((spread2, ch, all_goc), bf16),
            dma((2, nc)), dma((2, nc)), dma((2, nc)), dma((2, nc)), dma((2, nc)),
            dma((2, lanes)), dma((2, lanes)), dma((2, lanes)), dma((2, lanes)), dma((2, lanes)), dma((2, lanes)),
            pltpu.VMEM((every, planes, ch, cells), bf16),
            pltpu.VMEM((every, all_goc, ocells), bf16),
            pltpu.VMEM((4, all_goc, every * ocells), bf16),
            pltpu.VMEM((8, ch, every * ocells), bf16),
            dma((2, every)), dma((2, every)), dma((2, every)), dma((2, every * nc)),
        ],
        compiler_params=pltpu.CompilerParams(
            collective_id=0, has_side_effects=True, vmem_limit_bytes=48 * 1024 * 1024),
    )(x, h, g, w1, w2)
    in_grad = jnp.swapaxes(out, 0, 1).reshape(inputs.shape)
    return (in_grad, one.reshape(TAPS, TAPS, TAPS, ch, all_ch), two.reshape(TAPS, TAPS, TAPS, ch, all_goc))


def solution(mesh):
    in_specs = (
        P("groups", "chan", "space", None),
        P("groups", "chan", "space", None),
        P("groups", "chan", "space", None),
        P(None, None, None, "chan", None),
        P(None, None, None, "chan", None),
    )
    out_specs = (
        P("groups", "chan", "space", None),
        P("groups", None, None, "chan", None),
        P("groups", None, None, "chan", None),
    )
    body = functools.partial(shards, mesh.shape["chan"], mesh.shape["space"])
    return jax.shard_map(body, mesh=mesh, in_specs=in_specs, out_specs=out_specs, check_vma=False)
```
